512 devices in a mesh: seg: 16 (over z_lo, core), head: 32 (over z_hi, x, y).
Axes of the slice: x: 4, y: 4, z: 16 (z_hi: 2, z_lo: 8; z = z_hi * 8 + z_lo), core: 2. Of those that a mesh axis runs over, the one named last changes fastest.
Arguments:
- queries: bfloat16 [65536, 4096], P(('seg', 'head')), may hold values from -256 to 256
- latent_keys: bfloat16 [768, 4096], P('seg', 'head'), may hold values from -12 to 12
- latent_values: bfloat16 [768, 4096], P('seg', 'head'), may hold values from -6 to 6
- cotangent: bfloat16 [65536, 4096], P(('seg', 'head')), may hold values from -6 to 6
- gate_logits: float32 [32], P('head'), may hold values from 0.3 to 1.5
- visibility: int32 [512, 16], replicated, may hold values from 0 to 1, as said below
- text_counts: int32 [16], replicated, may hold values from 2048 to 4096, as said below
- latent_counts: int32 [16], replicated, may hold values from 2 to 48, as said below
Outputs:
- mixed_rows: bfloat16 [65536, 4096], P(('seg', 'head'))
- grad_queries: bfloat16 [65536, 4096], P(('seg', 'head'))
- grad_keys: bfloat16 [768, 4096], P('seg', 'head')
- grad_values: bfloat16 [768, 4096], P('seg', 'head')
The draws below stay inside these ranges and needn't reach their ends.
Inputs may be any that keep to these rules, and one draw needn't show every extreme that they name: `visibility`: in the text block's own segment the entry is 1, for later segments it is 0. `text_counts`: one segment has all 4096 rows valid and one has 2048. `latent_counts`: one segment has all 48 rows valid and one has 2.
All inputs are finite; a program needn't handle non-finite values.
Results may differ from the reference program's by a relative error of at most 0.019.
Values may be sent and summed in bfloat16 or wider, within the bound.
No kernel may reach another device: no remote copies, remote signals or barrier semaphores. Data moves between devices by JAX's collectives and lax.ppermute only.
A program may use at most 64 MiB of HBM per device.

```python
import math
import jax
import jax.numpy as jnp
from jax import lax

HD = 128
H = 32
LAT_SEG = 48
MB = 128
SEG_TOK = 4096
TOKENS = 65536
LAT = 768
NTB = 512


def key_table(base_key):
    table_key = jax.random.fold_in(base_key, 11)
    first_key, second_key = jax.random.split(table_key, 2)
    entries = jax.random.truncated_normal(first_key, -4.0, 4.0, (LAT, H * HD), jnp.float32)
    row_scale = jnp.exp(jax.random.uniform(second_key, (LAT, 1), jnp.float32, math.log(0.3), math.log(3.0)))
    table = entries * row_scale
    return table


def draw_latent_keys(key, part):
    return key_table(key).astype(jnp.bfloat16)


def draw_queries(key, part):
    query_key = jax.random.fold_in(key, 23)
    first_key = jax.random.fold_in(query_key, 0)
    table = jax.random.truncated_normal(first_key, -4.0, 4.0, (TOKENS, H * HD), jnp.float32)
    return table.astype(jnp.bfloat16)


def draw_visibility(key, part):
    seg_total = LAT // LAT_SEG
    coin_flips = jax.random.randint(jax.random.fold_in(key, 31), (NTB, seg_total), 0, 2)
    text_seg = jnp.arange(NTB, dtype=jnp.int32) * MB // SEG_TOK
    latent_seg = jnp.arange(seg_total, dtype=jnp.int32)
    earlier = latent_seg[None, :] < text_seg[:, None]
    same_seg = latent_seg[None, :] == text_seg[:, None]
    return jnp.where(same_seg, 1, jnp.where(earlier, coin_flips, 0)).astype(jnp.int32)


def ragged_counts(base_key, low_count, high_count):
    seg_total = LAT // LAT_SEG
    first_key, second_key = jax.random.split(base_key)
    counts = jax.random.randint(first_key, (seg_total,), low_count, high_count + 1)
    picked = jax.random.permutation(second_key, seg_total)
    counts = counts.at[picked[0]].set(high_count).at[picked[1]].set(low_count)
    return counts.astype(jnp.int32)


def draw_text_counts(key, part):
    return ragged_counts(jax.random.fold_in(key, 41), SEG_TOK // 2, SEG_TOK)


def draw_latent_counts(key, part):
    return ragged_counts(jax.random.fold_in(key, 43), 2, LAT_SEG)


def level_of(key, shape, shards, smallest, largest):
    loudness = 1.0
    for dim, parts in shards:
        heights = jax.random.uniform(jax.random.fold_in(jax.random.fold_in(key, 6), dim), (parts,), jnp.float32, smallest / len(shards), largest / len(shards))
        loudness = loudness * jnp.repeat(jnp.exp(heights), shape[dim] // parts).reshape((-1,) + (1,) * (len(shape) - 1 - dim))
    return loudness


def noise(rng, extent, deviation, bound, shards=(), kind=jnp.bfloat16):
    factor_of = level_of(rng, extent, shards, -0.22, 0.18) if shards else 1.0
    values = jax.random.normal(rng, extent, jnp.float32) * deviation * factor_of
    return jnp.minimum(jnp.maximum(values, -bound), bound).astype(kind)


def setup_inputs(seed: int = 0) -> dict:
    key_of = jax.random.split(jax.random.key(seed), 9)
    queries = draw_queries(jax.random.fold_in(key_of[8], 71), 0)
    latent_keys = draw_latent_keys(jax.random.fold_in(key_of[8], 71), 0)
    latent_values = noise(key_of[2], (LAT, H * HD), 1.0, 6.0, ((0, 16), (1, 32)))
    cotangent = noise(key_of[3], (TOKENS, H * HD), 1.0, 6.0, ((0, 512),))
    gate_logits = jnp.clip(0.3 + 1.2 * jax.random.uniform(key_of[4], (H,), jnp.float32) ** level_of(key_of[4], (H,), ((0, 32),), -0.2, 0.2), 0.3, 1.5)
    visibility = draw_visibility(jax.random.fold_in(key_of[8], 71), 0)
    text_counts = draw_text_counts(jax.random.fold_in(key_of[8], 71), 0)
    latent_counts = draw_latent_counts(jax.random.fold_in(key_of[8], 71), 0)
    return dict(queries=queries, latent_keys=latent_keys, latent_values=latent_values, cotangent=cotangent, gate_logits=gate_logits, visibility=visibility, text_counts=text_counts, latent_counts=latent_counts)


def head_terms(query_head, key_head, value_head, grad_head, tanh_gate, seen_full, valid_rows):
    scaling = 1.0 / math.sqrt(HD)
    block_rows = math.gcd(TOKENS, 1024)
    block_count = TOKENS // block_rows
    block_masks = block_rows // MB
    block_inputs = (query_head.reshape(block_count, block_rows, HD), grad_head.reshape(block_count, block_rows, HD), seen_full.reshape(block_count, block_masks, LAT), valid_rows.reshape(block_count, block_rows))

    def row_step(running, pieces):
        key_sum, value_sum = running
        query_rows, grad_rows, seen_block, valid_block = pieces
        visible = jnp.broadcast_to(seen_block[:, None, :], (block_masks, MB, LAT)).reshape(block_rows, LAT)
        scores = jnp.dot(query_rows, key_head.T, preferred_element_type=jnp.float32) * scaling
        masked = jnp.where(visible, scores, -1e+30)
        row_top = lax.optimization_barrier(jnp.max(masked, axis=1, keepdims=True))
        row_total = lax.optimization_barrier(jnp.sum(jnp.where(visible, jnp.exp(scores - row_top), 0.0), axis=1, keepdims=True))
        log_total = row_top + jnp.log(row_total)
        weights = jnp.where(visible, jnp.exp(scores - log_total), 0.0).astype(jnp.bfloat16)
        attended = jnp.dot(weights, value_head, preferred_element_type=jnp.float32).astype(jnp.bfloat16)
        gated_rows = (valid_block[:, None] * tanh_gate * attended.astype(jnp.float32)).astype(jnp.bfloat16)
        grad_output = (valid_block[:, None] * tanh_gate * grad_rows.astype(jnp.float32)).astype(jnp.bfloat16)
        row_delta = lax.optimization_barrier(jnp.sum(grad_output.astype(jnp.float32) * attended.astype(jnp.float32), axis=1, keepdims=True))
        grad_weights = jnp.dot(grad_output, value_head.T, preferred_element_type=jnp.float32)
        grad_scores = (weights.astype(jnp.float32) * (grad_weights - row_delta) * scaling).astype(jnp.bfloat16)
        grad_query = jnp.dot(grad_scores, key_head, preferred_element_type=jnp.float32).astype(jnp.bfloat16)
        key_sum = key_sum + jnp.dot(grad_scores.T, query_rows, preferred_element_type=jnp.float32)
        value_sum = value_sum + jnp.dot(weights.T, grad_output, preferred_element_type=jnp.float32)
        return ((key_sum, value_sum), (gated_rows, grad_query))
    zero_sums = jnp.zeros((LAT, HD), jnp.float32)
    (key_sum, value_sum), (gated_all, grad_all) = lax.scan(row_step, (zero_sums, zero_sums), block_inputs)
    return (gated_all.reshape(TOKENS, HD), grad_all.reshape(TOKENS, HD), key_sum.astype(jnp.bfloat16), value_sum.astype(jnp.bfloat16))

def reference(queries, latent_keys, latent_values, cotangent, gate_logits, visibility, text_counts, latent_counts):
    tok_rows = jnp.arange(TOKENS, dtype=jnp.int32)
    valid_rows = (tok_rows % SEG_TOK < text_counts[tok_rows // SEG_TOK]).astype(jnp.float32)
    slot_ok = latent_counts[:, None] > jnp.arange(LAT_SEG, dtype=jnp.int32)[None, :]
    seen_full = ((visibility[:, :, None] > 0) & slot_ok[None, :, :]).reshape(NTB, LAT)
    gate_values = jnp.tanh(gate_logits)

    def per_head(head_index):
        column_start = (head_index * HD).astype(jnp.int32)
        query_head = lax.dynamic_slice_in_dim(queries, column_start, HD, 1)
        key_head = lax.dynamic_slice_in_dim(latent_keys, column_start, HD, 1)
        value_head = lax.dynamic_slice_in_dim(latent_values, column_start, HD, 1)
        grad_head = lax.dynamic_slice_in_dim(cotangent, column_start, HD, 1)
        return head_terms(query_head, key_head, value_head, grad_head, gate_values[head_index], seen_full, valid_rows)
    gated, grad_q, grad_k, grad_v = lax.map(per_head, jnp.arange(H, dtype=jnp.int32))
    mixed_rows = gated.transpose(1, 0, 2).reshape(TOKENS, H * HD)
    grad_queries = grad_q.transpose(1, 0, 2).reshape(TOKENS, H * HD)
    grad_keys = grad_k.transpose(1, 0, 2).reshape(LAT, H * HD)
    grad_values = grad_v.transpose(1, 0, 2).reshape(LAT, H * HD)
    return (mixed_rows, grad_queries, grad_keys, grad_values)
```

```python
import functools
import math

import jax
import jax.numpy as jnp
from jax import lax
from jax.experimental import pallas as pl
from jax.experimental.pallas import tpu as pltpu
from jax.sharding import Mesh
from jax.sharding import PartitionSpec as P

MB = 128
HIDDEN = -1e30
GATE_ROWS = 8


def spread_kernel(query_ref, grad_ref, *piece_refs):
    peers = piece_refs[0].shape[0]
    width = piece_refs[0].shape[3]
    for half, piece_ref in enumerate(piece_refs):
        for peer in range(peers):
            columns = pl.ds((half * peers + peer) * width, width)
            piece_ref[peer, 0] = query_ref[:, columns]
            piece_ref[peer, 1] = grad_ref[:, columns]


def spread(queries, cotangent, halves, peers):
    rows, columns = queries.shape
    width = columns // (halves * peers)
    piece = jax.ShapeDtypeStruct((peers, 2, rows, width), queries.dtype)
    return pl.pallas_call(
        spread_kernel,
        out_shape=[piece] * halves,
        name="spread",
        cost_estimate=pl.CostEstimate(
            flops=0, bytes_accessed=8 * rows * columns, transcendentals=0
        ),
    )(queries, cotangent)


def collect_kernel(*refs):
    *piece_refs, mixed_ref, grad_ref = refs
    peers = piece_refs[0].shape[0]
    width = piece_refs[0].shape[3]
    for half, piece_ref in enumerate(piece_refs):
        for peer in range(peers):
            columns = pl.ds((half * peers + peer) * width, width)
            mixed_ref[:, columns] = piece_ref[peer, 0]
            grad_ref[:, columns] = piece_ref[peer, 1]


def collect(pieces):
    peers, _, rows, width = pieces[0].shape
    columns = len(pieces) * peers * width
    whole = jax.ShapeDtypeStruct((rows, columns), pieces[0].dtype)
    return pl.pallas_call(
        collect_kernel,
        out_shape=[whole, whole],
        name="collect",
        cost_estimate=pl.CostEstimate(
            flops=0, bytes_accessed=8 * rows * columns, transcendentals=0
        ),
    )(*pieces)


def head_kernel(
    half,
    scalars_ref,
    latent_ref,
    visible_ref,
    text_ref,
    out_ref,
    latent_grad_ref,
    key_ref,
    value_ref,
    key_turned_ref,
    value_turned_ref,
    gate_ref,
    key_sum_ref,
    value_sum_ref,
):
    step = pl.program_id(0)
    groups, _, rows, dim = text_ref.shape
    segments, seg_rows, _ = latent_ref.shape
    slots = seg_rows - GATE_ROWS
    lanes = visible_ref.shape[1]
    block_rows = groups * rows
    scaling = 1.0 / math.sqrt(dim)
    to_power = scaling * math.log2(math.e)

    @pl.when(step == 0)
    def _():
        for s in range(segments):
            at = pl.ds(s * slots, slots)
            key_ref[at, :dim] = latent_ref[s, :slots, :dim]
            value_ref[at, :] = latent_ref[s, :slots, dim:]
            slot_ok = lax.broadcasted_iota(jnp.int32, (slots, lanes), 0) < scalars_ref[2 + s]
            seen = jnp.broadcast_to(visible_ref[s : s + 1, :] > 0, (slots, lanes))
            key_ref[at, dim:] = jnp.where(slot_ok & seen, 0.0, HIDDEN).astype(jnp.bfloat16)
        key_turned_ref[...] = key_ref[:, :dim].astype(jnp.float32).T.astype(jnp.bfloat16)
        value_turned_ref[...] = value_ref[...].astype(jnp.float32).T.astype(jnp.bfloat16)
        parts = latent_ref[0, slots:, :dim].astype(jnp.float32)[0:1, :]
        gate_ref[...] = jnp.tanh(jnp.broadcast_to(jnp.sum(parts, axis=1, keepdims=True), (1, dim)))
        key_sum_ref[...] = jnp.zeros_like(key_sum_ref)
        value_sum_ref[...] = jnp.zeros_like(value_sum_ref)

    own_count = scalars_ref[0]
    first_block = scalars_ref[1]
    first_row = step * block_rows
    gate = gate_ref[...]
    valid_column = (
        lax.broadcasted_iota(jnp.int32, (block_rows, dim), 0) + first_row < own_count
    )
    valid_row = (
        lax.broadcasted_iota(jnp.int32, (dim, block_rows), 1) + first_row < own_count
    )
    query = text_ref[:, 0].reshape(block_rows, dim)
    grad = text_ref[:, 1].reshape(block_rows, dim)
    grad_wide = jnp.where(valid_column, grad.astype(jnp.float32) * gate, 0.0)
    grad_out = grad_wide.astype(jnp.bfloat16)
    block_of = lax.broadcasted_iota(jnp.int32, (groups, rows, lanes), 0).reshape(block_rows, lanes)
    lane_of = lax.broadcasted_iota(jnp.int32, (block_rows, lanes), 1)
    pick = jnp.where(lane_of == block_of + (first_block + step * groups), 1.0, 0.0)
    asked = jnp.concatenate([query, pick.astype(jnp.bfloat16)], axis=1)
    turned = (((1,), (1,)), ((), ()))
    scores = lax.dot_general(key_ref[...], asked, turned, preferred_element_type=jnp.float32)
    top = jnp.max(scores, axis=0, keepdims=True)
    powers = jnp.exp2((scores - top) * to_power)
    total = jnp.sum(powers, axis=0, keepdims=True)
    weights = (powers * (1.0 / total)).astype(jnp.bfloat16)
    attended = jnp.dot(value_turned_ref[...], weights, preferred_element_type=jnp.float32)
    attended = attended.astype(jnp.bfloat16).astype(jnp.float32)
    gate_scalar = gate[:, 0:1]
    mixed = jnp.where(valid_row, attended * gate_scalar, 0.0)
    out_ref[:, 0] = mixed.T.astype(jnp.bfloat16).reshape(groups, rows, dim)
    grad_turned = grad_out.astype(jnp.float32).T
    delta = jnp.sum(grad_turned * attended, axis=0, keepdims=True)
    grad_weights = jnp.dot(
        value_ref[...], grad_turned.astype(jnp.bfloat16), preferred_element_type=jnp.float32
    )
    grad_scores = (weights.astype(jnp.float32) * (grad_weights - delta)).astype(jnp.bfloat16)
    grad_query = (
        jnp.dot(key_turned_ref[...], grad_scores, preferred_element_type=jnp.float32) * scaling
    )
    out_ref[:, 1] = grad_query.T.astype(jnp.bfloat16).reshape(groups, rows, dim)
    key_sum_ref[...] += jnp.dot(grad_scores, query, preferred_element_type=jnp.float32)
    value_sum_ref[...] += jnp.dot(weights, grad_out, preferred_element_type=jnp.float32)

    @pl.when(step == pl.num_programs(0) - 1)
    def _():
        for s in range(segments):
            at = pl.ds(s * slots, slots)
            latent_grad_ref[s % 2, s // 2, :, :dim] = (key_sum_ref[at, :] * scaling).astype(
                jnp.bfloat16
            )
            latent_grad_ref[s % 2, s // 2, :, dim:] = value_sum_ref[at, :].astype(jnp.bfloat16)


def head_pass(half, scalars, visible_turned, latents, text, groups):
    peers, _, rows, dim = text.shape
    segments, seg_rows, _ = latents.shape
    slots = seg_rows - GATE_ROWS
    lat = segments * slots
    lanes = 128
    text_rows = peers * rows
    grid_spec = pltpu.PrefetchScalarGridSpec(
        num_scalar_prefetch=1,
        grid=(peers // groups,),
        in_specs=[
            pl.BlockSpec((segments, seg_rows, 2 * dim), lambda i, s: (0, 0, 0)),
            pl.BlockSpec((segments, lanes), lambda i, s: (0, s[2 + segments])),
            pl.BlockSpec((groups, 2, rows, dim), lambda i, s: (i, 0, 0, 0)),
        ],
        out_specs=[
            pl.BlockSpec((groups, 2, rows, dim), lambda i, s: (i, 0, 0, 0)),
            pl.BlockSpec((2, segments // 2, slots, 2 * dim), lambda i, s: (0, 0, 0, 0)),
        ],
        scratch_shapes=[
            pltpu.VMEM((lat, dim + lanes), jnp.bfloat16),
            pltpu.VMEM((lat, dim), jnp.bfloat16),
            pltpu.VMEM((dim, lat), jnp.bfloat16),
            pltpu.VMEM((dim, lat), jnp.bfloat16),
            pltpu.VMEM((1, dim), jnp.float32),
            pltpu.VMEM((lat, dim), jnp.float32),
            pltpu.VMEM((lat, dim), jnp.float32),
        ],
    )
    return pl.pallas_call(
        functools.partial(head_kernel, half),
        grid_spec=grid_spec,
        out_shape=[
            jax.ShapeDtypeStruct((peers, 2, rows, dim), jnp.bfloat16),
            jax.ShapeDtypeStruct((2, segments // 2, slots, 2 * dim), jnp.bfloat16),
        ],
        name="head_pass",
        compiler_params=pltpu.CompilerParams(vmem_limit_bytes=48 << 20),
        cost_estimate=pl.CostEstimate(
            flops=12 * text_rows * lat * dim,
            bytes_accessed=8 * text_rows * dim + 8 * lat * dim,
            transcendentals=text_rows * lat,
        ),
    )(scalars, latents, visible_turned, text)


def shards(
    queries,
    latent_keys,
    latent_values,
    cotangent,
    gate_logits,
    visibility,
    text_counts,
    latent_counts,
):
    halves = lax.axis_size("z_hi")
    peers = lax.axis_size("x") * lax.axis_size("y")
    seg_count = latent_counts.shape[0]
    seg_index = lax.axis_index("z_lo") * lax.axis_size("core") + lax.axis_index("core")
    half_index = lax.axis_index("z_hi")
    rows = queries.shape[0]
    slots, dim = latent_keys.shape

    pieces = spread(queries, cotangent, halves, peers)
    texts = [lax.all_to_all(p, ("x", "y"), split_axis=0, concat_axis=0, tiled=True) for p in pieces]

    first = lax.reduce_precision(gate_logits, 8, 7)
    second = lax.reduce_precision(gate_logits - first, 8, 7)
    third = gate_logits - first - second
    terms = jnp.concatenate([first, second, third]).astype(jnp.bfloat16)
    gate_tile = jnp.pad(terms[None, :], ((0, GATE_ROWS - 1), (0, 2 * dim - 3)))
    packed = jnp.concatenate(
        [jnp.concatenate([latent_keys, latent_values], axis=1), gate_tile], axis=0
    )
    latents = lax.all_gather(packed[None], "core", axis=0, tiled=True)
    latents = lax.all_gather(latents, ("z_hi", "z_lo"), axis=0, tiled=True)
    latents = latents.reshape(halves, seg_count, slots + GATE_ROWS, 2 * dim)

    half_blocks = peers * rows // MB
    first_block = (seg_index * halves + half_index) * half_blocks
    own_count = lax.dynamic_index_in_dim(text_counts, seg_index, keepdims=False)
    own_count = own_count - half_index * peers * rows
    scalars = jnp.concatenate(
        [
            jnp.stack([own_count, first_block % 128]).astype(jnp.int32),
            latent_counts,
            jnp.stack([first_block // 128]).astype(jnp.int32),
        ]
    )
    visible_turned = visibility.T

    outs, latent_grads = [], []
    for half in range(halves):
        out, latent_grad = head_pass(
            half, scalars, visible_turned, latents[half], texts[half], groups=4
        )
        outs.append(lax.all_to_all(out, ("x", "y"), split_axis=0, concat_axis=0, tiled=True))
        latent_grads.append(latent_grad)

    both = jnp.stack(latent_grads, axis=1)
    swapped = lax.all_to_all(both, "core", split_axis=0, concat_axis=0, tiled=True)
    summed = jnp.sum(swapped.astype(jnp.float32), axis=0).astype(jnp.bfloat16)
    summed = summed.reshape(halves * (seg_count // 2), slots, 2 * dim)
    shared = lax.all_to_all(summed, ("z_hi", "z_lo"), split_axis=0, concat_axis=0, tiled=True)
    final = jnp.sum(shared.astype(jnp.float32), axis=0).astype(jnp.bfloat16)
    mixed_rows, grad_queries = collect(outs)
    return (mixed_rows, grad_queries, final[:, :dim], final[:, dim:])


def solution(mesh):
    fine = Mesh(mesh.devices.reshape(8, 2, 2, 4, 4), ("z_lo", "core", "z_hi", "x", "y"))
    seg, head = ("z_lo", "core"), ("z_hi", "x", "y")
    in_specs = (
        P(seg + head, None),
        P(seg, head),
        P(seg, head),
        P(seg + head, None),
        P(head),
        P(),
        P(),
        P(),
    )
    out_specs = (P(seg + head, None), P(seg + head, None), P(seg, head), P(seg, head))
    return jax.shard_map(shards, mesh=fine, in_specs=in_specs, out_specs=out_specs, check_vma=False)
```

```python
import math

import jax
import jax.numpy as jnp
from jax import lax
from jax.experimental import pallas as pl
from jax.experimental.pallas import tpu as pltpu
from jax.sharding import Mesh
from jax.sharding import PartitionSpec as P


MB = 128
HIDDEN = -1e30
GATE_ROWS = 8
NEAR = 4


def spread_kernel(gate_ref, query_ref, grad_ref, latent_key_ref, latent_value_ref, text_ref, packed_ref):
    peers, _, _, width = text_ref.shape
    for peer in range(peers):
        columns = pl.ds(peer * width, width)
        text_ref[peer, 0] = query_ref[:, columns]
        text_ref[peer, 1] = grad_ref[:, columns]

    @pl.when(pl.program_id(0) == 0)
    def _():
        slots, dim = latent_key_ref.shape
        packed_ref[:slots, :dim] = latent_key_ref[...]
        packed_ref[:slots, dim:] = latent_value_ref[...]
        gate = jnp.full((GATE_ROWS, 2 * dim), gate_ref[0], jnp.float32)
        first = gate.astype(jnp.bfloat16).astype(jnp.float32)
        second = (gate - first).astype(jnp.bfloat16).astype(jnp.float32)
        third = gate - first - second
        lane = lax.broadcasted_iota(jnp.int32, gate.shape, 1)
        terms = jnp.where(lane == 0, first, jnp.where(lane == 1, second, third))
        packed_ref[slots:, :] = jnp.where(lane < 3, terms, 0.0).astype(jnp.bfloat16)


def spread(gate_logits, queries, cotangent, latent_keys, latent_values, halves, peers):
    rows, columns = queries.shape
    width = columns // (halves * peers)
    slots, dim = latent_keys.shape
    parts = 2
    chunk = columns // (halves * parts)
    whole = pl.BlockSpec((slots, dim), lambda i: (0, 0))
    return pl.pallas_call(
        spread_kernel,
        grid=(halves * parts,),
        in_specs=[
            pl.BlockSpec(memory_space=pltpu.SMEM),
            pl.BlockSpec((rows, chunk), lambda i: (0, i)),
            pl.BlockSpec((rows, chunk), lambda i: (0, i)),
            whole,
            whole,
        ],
        out_specs=[
            pl.BlockSpec((peers // parts, 2, rows, width), lambda i: (i % parts, i // parts, 0, 0)),
            pl.BlockSpec((slots + GATE_ROWS, 2 * dim), lambda i: (0, 0)),
        ],
        out_shape=[
            jax.ShapeDtypeStruct((peers, 2 * halves, rows, width), queries.dtype),
            jax.ShapeDtypeStruct((slots + GATE_ROWS, 2 * dim), queries.dtype),
        ],
        name="spread",
        cost_estimate=pl.CostEstimate(
            flops=0, bytes_accessed=8 * rows * columns, transcendentals=0
        ),
    )(gate_logits, queries, cotangent, latent_keys, latent_values)


def collect_kernel(text_ref, mixed_ref, grad_ref):
    peers, _, _, width = text_ref.shape
    for peer in range(peers):
        columns = pl.ds(peer * width, width)
        mixed_ref[:, columns] = text_ref[peer, 0]
        grad_ref[:, columns] = text_ref[peer, 1]


def collect(text):
    peers, kinds, rows, width = text.shape
    halves = kinds // 2
    columns = halves * peers * width
    parts = 2
    whole = jax.ShapeDtypeStruct((rows, columns), text.dtype)
    block = pl.BlockSpec((rows, columns // (halves * parts)), lambda i: (0, i))
    return pl.pallas_call(
        collect_kernel,
        grid=(halves * parts,),
        in_specs=[
            pl.BlockSpec((peers // parts, 2, rows, width), lambda i: (i % parts, i // parts, 0, 0))
        ],
        out_specs=[block, block],
        out_shape=[whole, whole],
        name="collect",
        cost_estimate=pl.CostEstimate(
            flops=0, bytes_accessed=8 * rows * columns, transcendentals=0
        ),
    )(text)


def heads_kernel(
    place_ref,
    text_counts_ref,
    latent_counts_ref,
    latent_ref,
    visible_ref,
    text_ref,
    out_ref,
    keep_ref,
    send_ref,
    key_ref,
    value_ref,
    key_turned_ref,
    value_turned_ref,
    gate_ref,
    key_sum_ref,
    value_sum_ref,
):
    step = pl.program_id(1)
    steps = pl.num_programs(1)
    groups, _, rows, dim = text_ref.shape
    cores, pairs, seg_rows, _ = latent_ref.shape
    segments = cores * pairs
    slots = seg_rows - GATE_ROWS
    lanes = visible_ref.shape[1]
    block_rows = groups * rows
    scaling = 1.0 / math.sqrt(dim)
    to_power = scaling * math.log2(math.e)
    seg_index = place_ref[0] // 2
    half_index = place_ref[0] % 2

    @pl.when(step == 0)
    def _():
        for s in range(segments):
            at = pl.ds(s * slots, slots)
            latent = latent_ref.at[s % cores, s // cores]
            key_ref[at, :dim] = latent[:slots, :dim]
            value_ref[at, :] = latent[:slots, dim:]
            slot_ok = lax.broadcasted_iota(jnp.int32, (slots, lanes), 0) < latent_counts_ref[s]
            seen = jnp.broadcast_to(visible_ref[s : s + 1, :] > 0, (slots, lanes))
            key_ref[at, dim:] = jnp.where(slot_ok & seen, 0.0, HIDDEN).astype(jnp.bfloat16)
        key_turned_ref[...] = key_ref[:, :dim].astype(jnp.float32).T.astype(jnp.bfloat16)
        value_turned_ref[...] = value_ref[...].astype(jnp.float32).T.astype(jnp.bfloat16)
        terms = latent_ref[0, 0, slots:, :dim].astype(jnp.float32)[0:1, :]
        gate_ref[...] = jnp.tanh(jnp.broadcast_to(jnp.sum(terms, axis=1, keepdims=True), (1, dim)))
        key_sum_ref[...] = jnp.zeros_like(key_sum_ref)
        value_sum_ref[...] = jnp.zeros_like(value_sum_ref)

    own_count = text_counts_ref[seg_index] - half_index * (steps * block_rows)
    first_block = (place_ref[0] * (steps * groups)) % lanes
    first_row = step * block_rows
    gate = gate_ref[...]
    valid_column = (
        lax.broadcasted_iota(jnp.int32, (block_rows, dim), 0) + first_row < own_count
    )
    valid_row = (
        lax.broadcasted_iota(jnp.int32, (dim, block_rows), 1) + first_row < own_count
    )
    query = text_ref[:, 0].reshape(block_rows, dim)
    grad = text_ref[:, 1].reshape(block_rows, dim)
    grad_wide = jnp.where(valid_column, grad.astype(jnp.float32) * gate, 0.0)
    grad_out = grad_wide.astype(jnp.bfloat16)
    block_of = lax.broadcasted_iota(jnp.int32, (groups, rows, lanes), 0).reshape(block_rows, lanes)
    lane_of = lax.broadcasted_iota(jnp.int32, (block_rows, lanes), 1)
    pick = jnp.where(lane_of == block_of + (first_block + step * groups), 1.0, 0.0)
    asked = jnp.concatenate([query, pick.astype(jnp.bfloat16)], axis=1)
    turned = (((1,), (1,)), ((), ()))
    scores = lax.dot_general(key_ref[...], asked, turned, preferred_element_type=jnp.float32)
    top = jnp.max(scores, axis=0, keepdims=True)
    powers = jnp.exp2((scores - top) * to_power)
    total = jnp.sum(powers, axis=0, keepdims=True)
    weights = (powers * (1.0 / total)).astype(jnp.bfloat16)
    attended = jnp.dot(value_turned_ref[...], weights, preferred_element_type=jnp.float32)
    attended = attended.astype(jnp.bfloat16).astype(jnp.float32)
    mixed = jnp.where(valid_row, attended * gate[:, 0:1], 0.0)
    out_ref[:, 0] = mixed.T.astype(jnp.bfloat16).reshape(groups, rows, dim)
    grad_turned = grad_out.astype(jnp.float32).T
    delta = jnp.sum(grad_turned * attended, axis=0, keepdims=True)
    grad_weights = jnp.dot(
        value_ref[...], grad_turned.astype(jnp.bfloat16), preferred_element_type=jnp.float32
    )
    grad_scores = (weights.astype(jnp.float32) * (grad_weights - delta)).astype(jnp.bfloat16)
    grad_query = (
        jnp.dot(key_turned_ref[...], grad_scores, preferred_element_type=jnp.float32) * scaling
    )
    out_ref[:, 1] = grad_query.T.astype(jnp.bfloat16).reshape(groups, rows, dim)
    key_sum_ref[...] += jnp.dot(grad_scores, query, preferred_element_type=jnp.float32)
    value_sum_ref[...] += jnp.dot(weights, grad_out, preferred_element_type=jnp.float32)

    @pl.when(step == steps - 1)
    def _():
        core_index = seg_index % cores
        pair_index = seg_index // cores
        for near in range(NEAR):
            for far in range(pairs // NEAR):
                pair = pair_index ^ (far * NEAR + near)
                for ref, core in ((keep_ref, core_index), (send_ref, 1 - core_index)):
                    at = pl.ds(pl.multiple_of((pair * cores + core) * slots, 8), slots)
                    ref[near, far, :, :dim] = (key_sum_ref[at, :] * scaling).astype(ref.dtype)
                    ref[near, far, :, dim:] = value_sum_ref[at, :].astype(ref.dtype)


def attend_heads(place, text_counts, latent_counts, latents, visible_turned, text, groups):
    peers, kinds, rows, dim = text.shape
    halves = kinds // 2
    cores, _, pairs, seg_rows, _ = latents.shape
    slots = seg_rows - GATE_ROWS
    lat = cores * pairs * slots
    lanes = 128
    steps = peers // groups
    fars = pairs // NEAR
    text_spec = pl.BlockSpec((groups, 2, rows, dim), lambda h, i, *s: (i, h, 0, 0))
    sum_spec = pl.BlockSpec(
        (NEAR, fars, slots, 2 * dim), lambda h, i, p, *s: (0, h ^ (p[0] % 2), 0, 0)
    )
    grid_spec = pltpu.PrefetchScalarGridSpec(
        num_scalar_prefetch=3,
        grid=(halves, steps),
        in_specs=[
            pl.BlockSpec(
                (cores, pl.Squeezed(), pairs, seg_rows, 2 * dim),
                lambda h, i, *s: (0, h, 0, 0, 0),
            ),
            pl.BlockSpec(
                (cores * pairs, lanes), lambda h, i, p, *s: (0, p[0] * peers * rows // MB // lanes)
            ),
            text_spec,
        ],
        out_specs=[text_spec, sum_spec, sum_spec],
        scratch_shapes=[
            pltpu.VMEM((lat, dim + lanes), jnp.bfloat16),
            pltpu.VMEM((lat, dim), jnp.bfloat16),
            pltpu.VMEM((dim, lat), jnp.bfloat16),
            pltpu.VMEM((dim, lat), jnp.bfloat16),
            pltpu.VMEM((1, dim), jnp.float32),
            pltpu.VMEM((lat, dim), jnp.float32),
            pltpu.VMEM((lat, dim), jnp.float32),
        ],
    )
    sums = (NEAR, halves * fars, slots, 2 * dim)
    return pl.pallas_call(
        heads_kernel,
        grid_spec=grid_spec,
        out_shape=[
            jax.ShapeDtypeStruct(text.shape, jnp.bfloat16),
            jax.ShapeDtypeStruct(sums, jnp.float32),
            jax.ShapeDtypeStruct(sums, jnp.bfloat16),
        ],
        name="attend_heads",
        compiler_params=pltpu.CompilerParams(vmem_limit_bytes=48 << 20),
        cost_estimate=pl.CostEstimate(
            flops=12 * halves * peers * rows * lat * dim,
            bytes_accessed=8 * halves * peers * rows * dim,
            transcendentals=halves * peers * rows * lat,
        ),
    )(place, text_counts, latent_counts, latents, visible_turned, text)


def add_up(keep, send):
    fars = keep.shape[1] // 2
    pairs = lax.axis_size("z_lo")
    other = lax.ppermute(send, "core", [(0, 1), (1, 0)])
    keep = keep + other.astype(jnp.float32)
    send = keep[1:].astype(jnp.bfloat16)
    keep = keep[0]
    arrived = []
    for near in range(1, NEAR):
        steps = [(i, i ^ near) for i in range(pairs)]
        arrived.append(lax.ppermute(send[near - 1], "z_lo", steps))
    for other in arrived:
        keep = keep + other.astype(jnp.float32)
    other = lax.ppermute(keep[fars:].astype(jnp.bfloat16), "z_hi", [(0, 1), (1, 0)])
    keep = keep[:fars] + other.astype(jnp.float32)
    steps = [(i, i ^ NEAR) for i in range(pairs)]
    other = lax.ppermute(keep[1].astype(jnp.bfloat16), "z_lo", steps)
    return (keep[0] + other.astype(jnp.float32)).astype(jnp.bfloat16)


def shards(
    queries,
    latent_keys,
    latent_values,
    cotangent,
    gate_logits,
    visibility,
    text_counts,
    latent_counts,
):
    halves = lax.axis_size("z_hi")
    peers = lax.axis_size("x") * lax.axis_size("y")
    dim = latent_keys.shape[1]
    place = lax.axis_index(("z_lo", "core", "z_hi")).astype(jnp.int32).reshape(1)
    text, packed = spread(
        gate_logits, queries, cotangent, latent_keys, latent_values, halves, peers
    )
    text = lax.all_to_all(text, ("x", "y"), split_axis=0, concat_axis=0, tiled=True)
    latents = lax.all_gather(packed, ("z_hi", "z_lo"), axis=0, tiled=True)
    latents = lax.all_gather(latents, "core", axis=0, tiled=True)
    latents = latents.reshape(lax.axis_size("core"), halves, lax.axis_size("z_lo"), *packed.shape)
    out, keep, send = attend_heads(
        place, text_counts, latent_counts, latents, visibility.T, text, groups=4
    )
    out = lax.all_to_all(out, ("x", "y"), split_axis=0, concat_axis=0, tiled=True)
    grads = add_up(keep, send)
    mixed_rows, grad_queries = collect(out)
    return (mixed_rows, grad_queries, grads[:, :dim], grads[:, dim:])


def solution(mesh):
    fine = Mesh(mesh.devices.reshape(8, 2, 2, 4, 4), ("z_lo", "core", "z_hi", "x", "y"))
    seg, head = ("z_lo", "core"), ("z_hi", "x", "y")
    in_specs = (
        P(seg + head, None),
        P(seg, head),
        P(seg, head),
        P(seg + head, None),
        P(head),
        P(),
        P(),
        P(),
    )
    out_specs = (P(seg + head, None), P(seg + head, None), P(seg, head), P(seg, head))
    return jax.shard_map(shards, mesh=fine, in_specs=in_specs, out_specs=out_specs, check_vma=False)
```

```python
import math

import jax
import jax.numpy as jnp
from jax import lax
from jax.experimental import pallas as pl
from jax.experimental.pallas import tpu as pltpu
from jax.sharding import Mesh
from jax.sharding import PartitionSpec as P


MB = 128
HIDDEN = -1e30
GATE_ROWS = 8
NEAR = 4


def spread_kernel(
    gate_ref,
    latent_key_ref,
    latent_value_ref,
    query_ref,
    grad_ref,
    text_ref,
    packed_ref,
    held_ref,
    in_sems,
    out_sems,
):
    peers, kinds, _, width = text_ref.shape
    halves = kinds // 2
    chunks = in_sems.shape[1]
    chunk = query_ref.shape[1] // chunks
    chunk_peers = halves * peers // chunks

    def bring(kind, c):
        columns = pl.ds(c * chunk, chunk)
        source = (query_ref, grad_ref)[kind].at[:, columns]
        return pltpu.make_async_copy(source, held_ref.at[kind, :, columns], in_sems.at[kind, c])

    def put(kind, head):
        half, peer = head // peers, head % peers
        return pltpu.make_async_copy(
            held_ref.at[kind, :, pl.ds(head * width, width)],
            text_ref.at[peer, 2 * half + kind],
            out_sems.at[kind, head],
        )

    for c in range(chunks):
        for kind in range(2):
            bring(kind, c).start()
    slots, dim = latent_key_ref.shape
    packed_ref[:slots, :dim] = latent_key_ref[...]
    packed_ref[:slots, dim:] = latent_value_ref[...]
    gate = jnp.full((GATE_ROWS, 2 * dim), gate_ref[0], jnp.float32)
    first = gate.astype(jnp.bfloat16).astype(jnp.float32)
    second = (gate - first).astype(jnp.bfloat16).astype(jnp.float32)
    third = gate - first - second
    lane = lax.broadcasted_iota(jnp.int32, gate.shape, 1)
    terms = jnp.where(lane == 0, first, jnp.where(lane == 1, second, third))
    packed_ref[slots:, :] = jnp.where(lane < 3, terms, 0.0).astype(jnp.bfloat16)
    for c in range(chunks):
        for kind in range(2):
            bring(kind, c).wait()
            for head in range(c * chunk_peers, (c + 1) * chunk_peers):
                put(kind, head).start()
    for head in range(halves * peers):
        for kind in range(2):
            put(kind, head).wait()


def spread(gate_logits, queries, cotangent, latent_keys, latent_values, halves, peers):
    rows, columns = queries.shape
    width = columns // (halves * peers)
    slots, dim = latent_keys.shape
    chunks = 4
    vmem = pl.BlockSpec(memory_space=pltpu.VMEM)
    anywhere = pl.BlockSpec(memory_space=pl.ANY)
    return pl.pallas_call(
        spread_kernel,
        in_specs=[pl.BlockSpec(memory_space=pltpu.SMEM), vmem, vmem, anywhere, anywhere],
        out_specs=[anywhere, vmem],
        out_shape=[
            jax.ShapeDtypeStruct((peers, 2 * halves, rows, width), queries.dtype),
            jax.ShapeDtypeStruct((slots + GATE_ROWS, 2 * dim), queries.dtype),
        ],
        scratch_shapes=[
            pltpu.VMEM((2, rows, columns), queries.dtype),
            pltpu.SemaphoreType.DMA((2, chunks)),
            pltpu.SemaphoreType.DMA((2, halves * peers)),
        ],
        name="spread",
        cost_estimate=pl.CostEstimate(
            flops=0, bytes_accessed=8 * rows * columns, transcendentals=0
        ),
    )(gate_logits, latent_keys, latent_values, queries, cotangent)


def collect_kernel(text_ref, mixed_ref, grad_ref):
    peers, kinds, _, width = text_ref.shape
    for half in range(kinds // 2):
        for peer in range(peers):
            columns = pl.ds((half * peers + peer) * width, width)
            mixed_ref[:, columns] = text_ref[peer, 2 * half]
            grad_ref[:, columns] = text_ref[peer, 2 * half + 1]


def collect(text):
    peers, kinds, rows, width = text.shape
    columns = kinds // 2 * peers * width
    whole = jax.ShapeDtypeStruct((rows, columns), text.dtype)
    return pl.pallas_call(
        collect_kernel,
        out_shape=[whole, whole],
        name="collect",
        cost_estimate=pl.CostEstimate(
            flops=0, bytes_accessed=8 * rows * columns, transcendentals=0
        ),
    )(text)


def heads_kernel(
    place_ref,
    text_counts_ref,
    latent_counts_ref,
    latent_ref,
    visible_ref,
    text_ref,
    out_ref,
    keep_ref,
    send_ref,
    key_ref,
    value_ref,
    key_turned_ref,
    value_turned_ref,
    gate_ref,
    key_sum_ref,
    value_sum_ref,
):
    step = pl.program_id(1)
    steps = pl.num_programs(1)
    groups, _, rows, dim = text_ref.shape
    cores, pairs, seg_rows, _ = latent_ref.shape
    segments = cores * pairs
    slots = seg_rows - GATE_ROWS
    lanes = visible_ref.shape[1]
    block_rows = groups * rows
    scaling = 1.0 / math.sqrt(dim)
    to_power = scaling * math.log2(math.e)
    seg_index = place_ref[0] // 2
    half_index = place_ref[0] % 2

    @pl.when(step == 0)
    def _():
        for s in range(segments):
            at = pl.ds(s * slots, slots)
            latent = latent_ref.at[s % cores, s // cores]
            key_ref[at, :dim] = latent[:slots, :dim]
            value_ref[at, :] = latent[:slots, dim:]
            slot_ok = lax.broadcasted_iota(jnp.int32, (slots, lanes), 0) < latent_counts_ref[s]
            seen = jnp.broadcast_to(visible_ref[s : s + 1, :] > 0, (slots, lanes))
            key_ref[at, dim:] = jnp.where(slot_ok & seen, 0.0, HIDDEN).astype(jnp.bfloat16)
        key_turned_ref[...] = key_ref[:, :dim].astype(jnp.float32).T.astype(jnp.bfloat16)
        value_turned_ref[...] = value_ref[...].astype(jnp.float32).T.astype(jnp.bfloat16)
        terms = latent_ref[0, 0, slots:, :dim].astype(jnp.float32)[0:1, :]
        gate_ref[...] = jnp.tanh(jnp.broadcast_to(jnp.sum(terms, axis=1, keepdims=True), (1, dim)))
        key_sum_ref[...] = jnp.zeros_like(key_sum_ref)
        value_sum_ref[...] = jnp.zeros_like(value_sum_ref)

    own_count = text_counts_ref[seg_index] - half_index * (steps * block_rows)
    first_block = (place_ref[0] * (steps * groups)) % lanes
    first_row = step * block_rows
    gate = gate_ref[...]
    valid_column = (
        lax.broadcasted_iota(jnp.int32, (block_rows, dim), 0) + first_row < own_count
    )
    valid_row = (
        lax.broadcasted_iota(jnp.int32, (dim, block_rows), 1) + first_row < own_count
    )
    query = text_ref[:, 0].reshape(block_rows, dim)
    grad = text_ref[:, 1].reshape(block_rows, dim)
    grad_wide = jnp.where(valid_column, grad.astype(jnp.float32) * gate, 0.0)
    grad_out = grad_wide.astype(jnp.bfloat16)
    block_of = lax.broadcasted_iota(jnp.int32, (groups, rows, lanes), 0).reshape(block_rows, lanes)
    lane_of = lax.broadcasted_iota(jnp.int32, (block_rows, lanes), 1)
    pick = jnp.where(lane_of == block_of + (first_block + step * groups), 1.0, 0.0)
    asked = jnp.concatenate([query, pick.astype(jnp.bfloat16)], axis=1)
    turned = (((1,), (1,)), ((), ()))
    scores = lax.dot_general(key_ref[...], asked, turned, preferred_element_type=jnp.float32)
    top = jnp.max(scores, axis=0, keepdims=True)
    powers = jnp.exp2((scores - top) * to_power)
    total = jnp.sum(powers, axis=0, keepdims=True)
    weights = (powers * (1.0 / total)).astype(jnp.bfloat16)
    attended = jnp.dot(value_turned_ref[...], weights, preferred_element_type=jnp.float32)
    attended = attended.astype(jnp.bfloat16).astype(jnp.float32)
    mixed = jnp.where(valid_row, attended * gate[:, 0:1], 0.0)
    out_ref[:, 0] = mixed.T.astype(jnp.bfloat16).reshape(groups, rows, dim)
    grad_turned = grad_out.astype(jnp.float32).T
    delta = jnp.sum(grad_turned * attended, axis=0, keepdims=True)
    grad_weights = jnp.dot(
        value_ref[...], grad_turned.astype(jnp.bfloat16), preferred_element_type=jnp.float32
    )
    grad_scores = (weights.astype(jnp.float32) * (grad_weights - delta)).astype(jnp.bfloat16)
    grad_query = (
        jnp.dot(key_turned_ref[...], grad_scores, preferred_element_type=jnp.float32) * scaling
    )
    out_ref[:, 1] = grad_query.T.astype(jnp.bfloat16).reshape(groups, rows, dim)
    key_sum_ref[...] += jnp.dot(grad_scores, query, preferred_element_type=jnp.float32)
    value_sum_ref[...] += jnp.dot(weights, grad_out, preferred_element_type=jnp.float32)

    @pl.when(step == steps - 1)
    def _():
        core_index = seg_index % cores
        pair_index = seg_index // cores
        for near in range(NEAR):
            for far in range(pairs // NEAR):
                pair = pair_index ^ (far * NEAR + near)
                for ref, core in ((keep_ref, core_index), (send_ref, 1 - core_index)):
                    at = pl.ds(pl.multiple_of((pair * cores + core) * slots, 8), slots)
                    ref[near, far, :, :dim] = (key_sum_ref[at, :] * scaling).astype(ref.dtype)
                    ref[near, far, :, dim:] = value_sum_ref[at, :].astype(ref.dtype)


def attend_heads(place, text_counts, latent_counts, latents, visible_turned, text, groups):
    peers, kinds, rows, dim = text.shape
    halves = kinds // 2
    cores, _, pairs, seg_rows, _ = latents.shape
    slots = seg_rows - GATE_ROWS
    lat = cores * pairs * slots
    lanes = 128
    steps = peers // groups
    fars = pairs // NEAR
    text_spec = pl.BlockSpec((groups, 2, rows, dim), lambda h, i, *s: (i, h, 0, 0))
    sum_spec = pl.BlockSpec(
        (NEAR, fars, slots, 2 * dim), lambda h, i, p, *s: (0, h ^ (p[0] % 2), 0, 0)
    )
    grid_spec = pltpu.PrefetchScalarGridSpec(
        num_scalar_prefetch=3,
        grid=(halves, steps),
        in_specs=[
            pl.BlockSpec(
                (cores, pl.Squeezed(), pairs, seg_rows, 2 * dim),
                lambda h, i, *s: (0, h, 0, 0, 0),
            ),
            pl.BlockSpec(
                (cores * pairs, lanes), lambda h, i, p, *s: (0, p[0] * peers * rows // MB // lanes)
            ),
            text_spec,
        ],
        out_specs=[text_spec, sum_spec, sum_spec],
        scratch_shapes=[
            pltpu.VMEM((lat, dim + lanes), jnp.bfloat16),
            pltpu.VMEM((lat, dim), jnp.bfloat16),
            pltpu.VMEM((dim, lat), jnp.bfloat16),
            pltpu.VMEM((dim, lat), jnp.bfloat16),
            pltpu.VMEM((1, dim), jnp.float32),
            pltpu.VMEM((lat, dim), jnp.float32),
            pltpu.VMEM((lat, dim), jnp.float32),
        ],
    )
    sums = (NEAR, halves * fars, slots, 2 * dim)
    return pl.pallas_call(
        heads_kernel,
        grid_spec=grid_spec,
        out_shape=[
            jax.ShapeDtypeStruct(text.shape, jnp.bfloat16),
            jax.ShapeDtypeStruct(sums, jnp.float32),
            jax.ShapeDtypeStruct(sums, jnp.bfloat16),
        ],
        name="attend_heads",
        compiler_params=pltpu.CompilerParams(vmem_limit_bytes=48 << 20),
        cost_estimate=pl.CostEstimate(
            flops=12 * halves * peers * rows * lat * dim,
            bytes_accessed=8 * halves * peers * rows * dim,
            transcendentals=halves * peers * rows * lat,
        ),
    )(place, text_counts, latent_counts, latents, visible_turned, text)


def add_up(keep, send):
    fars = keep.shape[1] // 2
    pairs = lax.axis_size("z_lo")
    other = lax.ppermute(send, "core", [(0, 1), (1, 0)])
    keep = keep + other.astype(jnp.float32)
    send = keep[1:].astype(jnp.bfloat16)
    keep = keep[0]
    arrived = []
    for near in range(1, NEAR):
        steps = [(i, i ^ near) for i in range(pairs)]
        arrived.append(lax.ppermute(send[near - 1], "z_lo", steps))
    for other in arrived:
        keep = keep + other.astype(jnp.float32)
    send = keep[1:].astype(jnp.bfloat16)
    arrived = []
    for far in (2, 1, 3):
        half, block = far // fars, far % fars
        steps = [
            (2 * i + h, 2 * (i ^ (block * NEAR)) + (h ^ half)) for i in range(pairs) for h in range(2)
        ]
        arrived.append(lax.ppermute(send[far - 1], ("z_lo", "z_hi"), steps))
    keep = keep[0]
    for other in arrived:
        keep = keep + other.astype(jnp.float32)
    return keep.astype(jnp.bfloat16)


def shards(
    queries,
    latent_keys,
    latent_values,
    cotangent,
    gate_logits,
    visibility,
    text_counts,
    latent_counts,
):
    halves = lax.axis_size("z_hi")
    peers = lax.axis_size("x") * lax.axis_size("y")
    dim = latent_keys.shape[1]
    place = lax.axis_index(("z_lo", "core", "z_hi")).astype(jnp.int32).reshape(1)
    text, packed = spread(
        gate_logits, queries, cotangent, latent_keys, latent_values, halves, peers
    )
    text = lax.all_to_all(text, ("x", "y"), split_axis=0, concat_axis=0, tiled=True)
    latents = lax.all_gather(packed, ("z_hi", "z_lo"), axis=0, tiled=True)
    latents = lax.all_gather(latents, "core", axis=0, tiled=True)
    latents = latents.reshape(lax.axis_size("core"), halves, lax.axis_size("z_lo"), *packed.shape)
    out, keep, send = attend_heads(
        place, text_counts, latent_counts, latents, visibility.T, text, groups=4
    )
    out = lax.all_to_all(out, ("x", "y"), split_axis=0, concat_axis=0, tiled=True)
    grads = add_up(keep, send)
    mixed_rows, grad_queries = collect(out)
    return (mixed_rows, grad_queries, grads[:, :dim], grads[:, dim:])


def solution(mesh):
    fine = Mesh(mesh.devices.reshape(8, 2, 2, 4, 4), ("z_lo", "core", "z_hi", "x", "y"))
    seg, head = ("z_lo", "core"), ("z_hi", "x", "y")
    in_specs = (
        P(seg + head, None),
        P(seg, head),
        P(seg, head),
        P(seg + head, None),
        P(head),
        P(),
        P(),
        P(),
    )
    out_specs = (P(seg + head, None), P(seg + head, None), P(seg, head), P(seg, head))
    return jax.shard_map(shards, mesh=fine, in_specs=in_specs, out_specs=out_specs, check_vma=False)
```

```python
import math

import jax
import jax.numpy as jnp
from jax import lax
from jax.experimental import pallas as pl
from jax.experimental.pallas import tpu as pltpu
from jax.sharding import Mesh
from jax.sharding import PartitionSpec as P


MB = 128
HIDDEN = -1e30
GATE_ROWS = 8
NEAR = 4
SUBS = 2
SIZES = (256, 384, 448, 512, 768)


def spread_kernel(
    gate_ref, query_ref, grad_ref, latent_key_ref, latent_value_ref, text_ref, packed_ref
):
    peers, kinds, _, width = text_ref.shape
    slots, dim = latent_key_ref.shape
    for half in range(kinds // 2):
        for peer in range(peers):
            columns = pl.ds((half * peers + peer) * width, width)
            text_ref[peer, 2 * half] = query_ref[:, columns]
            text_ref[peer, 2 * half + 1] = grad_ref[:, columns]
    packed_ref[:slots, :dim] = latent_key_ref[...]
    packed_ref[:slots, dim:] = latent_value_ref[...]
    gate = jnp.full((GATE_ROWS, 2 * dim), gate_ref[0], jnp.float32)
    first = gate.astype(jnp.bfloat16).astype(jnp.float32)
    second = (gate - first).astype(jnp.bfloat16).astype(jnp.float32)
    third = gate - first - second
    lane = lax.broadcasted_iota(jnp.int32, gate.shape, 1)
    terms = jnp.where(lane == 0, first, jnp.where(lane == 1, second, third))
    packed_ref[slots:, :] = jnp.where(lane < 3, terms, 0.0).astype(jnp.bfloat16)


def spread(gate_logits, queries, cotangent, latent_keys, latent_values, halves, peers):
    rows, columns = queries.shape
    width = columns // (halves * peers)
    slots, dim = latent_keys.shape
    vmem = pl.BlockSpec(memory_space=pltpu.VMEM)
    return pl.pallas_call(
        spread_kernel,
        in_specs=[pl.BlockSpec(memory_space=pltpu.SMEM), vmem, vmem, vmem, vmem],
        out_specs=[vmem, vmem],
        out_shape=[
            jax.ShapeDtypeStruct((peers, 2 * halves, rows, width), queries.dtype),
            jax.ShapeDtypeStruct((slots + GATE_ROWS, 2 * dim), queries.dtype),
        ],
        name="spread",
        cost_estimate=pl.CostEstimate(
            flops=0, bytes_accessed=8 * rows * columns, transcendentals=0
        ),
    )(gate_logits, queries, cotangent, latent_keys, latent_values)


def collect_kernel(text_ref, mixed_ref, grad_ref):
    peers, kinds, _, width = text_ref.shape
    for half in range(kinds // 2):
        for peer in range(peers):
            columns = pl.ds((half * peers + peer) * width, width)
            mixed_ref[:, columns] = text_ref[peer, 2 * half]
            grad_ref[:, columns] = text_ref[peer, 2 * half + 1]


def collect(text):
    peers, kinds, rows, width = text.shape
    columns = kinds // 2 * peers * width
    whole = jax.ShapeDtypeStruct((rows, columns), text.dtype)
    return pl.pallas_call(
        collect_kernel,
        out_shape=[whole, whole],
        name="collect",
        cost_estimate=pl.CostEstimate(
            flops=0, bytes_accessed=8 * rows * columns, transcendentals=0
        ),
    )(text)


def heads_kernel(
    place_ref,
    text_counts_ref,
    latent_counts_ref,
    latent_ref,
    visible_ref,
    text_ref,
    out_ref,
    keep_ref,
    send_ref,
    key_ref,
    value_ref,
    key_turned_ref,
    value_turned_ref,
    gate_ref,
    key_sum_ref,
    value_sum_ref,
    hidden_ref,
    starts_ref,
):
    step = pl.program_id(1)
    steps = pl.num_programs(1)
    groups, _, rows, dim = text_ref.shape
    cores, pairs, seg_rows, _ = latent_ref.shape
    segments = cores * pairs
    slots = seg_rows - GATE_ROWS
    lanes = visible_ref.shape[1]
    block_rows = groups * rows
    scaling = 1.0 / math.sqrt(dim)
    to_power = scaling * math.log2(math.e)
    seg_index = place_ref[0] // 2
    half_index = place_ref[0] % 2

    @pl.when(step == 0)
    def _():
        key_sum_ref[...] = jnp.zeros_like(key_sum_ref)
        value_sum_ref[...] = jnp.zeros_like(value_sum_ref)
        hidden_ref[...] = jnp.full(hidden_ref.shape, HIDDEN, jnp.float32)
        start = 0
        for s in range(segments):
            at = pl.ds(start, slots)
            latent = latent_ref.at[s % cores, s // cores]
            count = jnp.where(s <= seg_index, latent_counts_ref[s], 0)
            key_sum_ref[at, :] = latent[:slots, :dim].astype(jnp.float32)
            value_sum_ref[at, :] = latent[:slots, dim:].astype(jnp.float32)
            slot_ok = lax.broadcasted_iota(jnp.int32, (slots, lanes), 0) < count
            seen = jnp.broadcast_to(visible_ref[s : s + 1, :] > 0, (slots, lanes))
            hidden_ref[at, :] = jnp.where(slot_ok & seen, 0.0, HIDDEN)
            starts_ref[s] = jnp.asarray(start, jnp.int32)
            start = start + count
        starts_ref[segments] = start
        key_ref[:, :dim] = key_sum_ref[...].astype(jnp.bfloat16)
        key_ref[:, dim:] = hidden_ref[...].astype(jnp.bfloat16)
        value_ref[...] = value_sum_ref[...].astype(jnp.bfloat16)
        key_turned_ref[...] = key_sum_ref[...].T.astype(jnp.bfloat16)
        value_turned_ref[...] = value_sum_ref[...].T.astype(jnp.bfloat16)
        terms = latent_ref[0, 0, slots:, :dim].astype(jnp.float32)[0:1, :]
        gate_ref[...] = jnp.tanh(jnp.broadcast_to(jnp.sum(terms, axis=1, keepdims=True), (1, dim)))
        key_sum_ref[...] = jnp.zeros_like(key_sum_ref)
        value_sum_ref[...] = jnp.zeros_like(value_sum_ref)

    own_count = text_counts_ref[seg_index] - half_index * (steps * block_rows)
    first_block = (place_ref[0] * (steps * groups)) % lanes
    first_row = step * block_rows
    gate = gate_ref[...]
    turned = (((1,), (1,)), ((), ()))
    sub_groups = groups // SUBS
    sub_rows = sub_groups * rows
    block_of = lax.broadcasted_iota(jnp.int32, (sub_groups, rows, lanes), 0)
    block_of = block_of.reshape(sub_rows, lanes)
    lane_of = lax.broadcasted_iota(jnp.int32, (sub_rows, lanes), 1)
    column_of = lax.broadcasted_iota(jnp.int32, (sub_rows, dim), 0)
    row_of = lax.broadcasted_iota(jnp.int32, (dim, sub_rows), 1)

    def score(sub, size):
        query = text_ref[sub * sub_groups : (sub + 1) * sub_groups, 0].reshape(sub_rows, dim)
        own_block = block_of + (first_block + step * groups + sub * sub_groups)
        pick = jnp.where(lane_of == own_block, 1.0, 0.0)
        asked = jnp.concatenate([query, pick.astype(jnp.bfloat16)], axis=1)
        return lax.dot_general(key_ref[:size], asked, turned, preferred_element_type=jnp.float32)

    def weigh(scores):
        top = jnp.max(scores, axis=0, keepdims=True)
        powers = jnp.exp2((scores - top) * to_power)
        total = jnp.sum(powers, axis=0, keepdims=True)
        return (powers * (1.0 / total)).astype(jnp.bfloat16)

    def finish(sub, size, weights):
        at = slice(sub * sub_groups, (sub + 1) * sub_groups)
        first = first_row + sub * sub_rows
        query = text_ref[at, 0].reshape(sub_rows, dim)
        grad = text_ref[at, 1].reshape(sub_rows, dim)
        valid_column = column_of + first < own_count
        valid_row = row_of + first < own_count
        grad_wide = jnp.where(valid_column, grad.astype(jnp.float32) * gate, 0.0)
        grad_out = grad_wide.astype(jnp.bfloat16)
        attended = jnp.dot(
            value_turned_ref[:, :size], weights, preferred_element_type=jnp.float32
        )
        attended = attended.astype(jnp.bfloat16).astype(jnp.float32)
        mixed = jnp.where(valid_row, attended * gate[:, 0:1], 0.0)
        out_ref[at, 0] = mixed.T.astype(jnp.bfloat16).reshape(sub_groups, rows, dim)
        grad_turned = grad_out.astype(jnp.float32).T
        delta = jnp.sum(grad_turned * attended, axis=0, keepdims=True)
        grad_weights = jnp.dot(
            value_ref[:size], grad_turned.astype(jnp.bfloat16), preferred_element_type=jnp.float32
        )
        grad_scores = weights * (grad_weights - delta).astype(jnp.bfloat16)
        grad_query = (
            jnp.dot(key_turned_ref[:, :size], grad_scores, preferred_element_type=jnp.float32)
            * scaling
        )
        out_ref[at, 1] = grad_query.T.astype(jnp.bfloat16).reshape(sub_groups, rows, dim)
        key_sum_ref[:size] += jnp.dot(grad_scores, query, preferred_element_type=jnp.float32)
        value_sum_ref[:size] += jnp.dot(weights, grad_out, preferred_element_type=jnp.float32)

    seen_latents = starts_ref[segments]
    for smaller, size in zip((0,) + SIZES, SIZES):

        @pl.when((seen_latents > smaller) & (seen_latents <= size))
        def _():
            ahead = score(0, size)
            for sub in range(SUBS):
                weights = weigh(ahead)
                if sub + 1 < SUBS:
                    ahead = score(sub + 1, size)
                finish(sub, size, weights)

    @pl.when(step == steps - 1)
    def _():
        core_index = seg_index % cores
        pair_index = seg_index // cores
        slot = lax.broadcasted_iota(jnp.int32, (slots, dim), 0)
        for near in range(NEAR):
            for far in range(pairs // NEAR):
                pair = pair_index ^ (far * NEAR + near)
                for ref, core in ((keep_ref, core_index), (send_ref, 1 - core_index)):
                    segment = pair * cores + core
                    at = pl.ds(starts_ref[segment], slots)
                    own = slot < starts_ref[segment + 1] - starts_ref[segment]
                    key_part = jnp.where(own, key_sum_ref[at, :] * scaling, 0.0)
                    value_part = jnp.where(own, value_sum_ref[at, :], 0.0)
                    ref[near, far, :, :dim] = key_part.astype(ref.dtype)
                    ref[near, far, :, dim:] = value_part.astype(ref.dtype)


def attend_heads(place, text_counts, latent_counts, latents, visible_turned, text, groups):
    peers, kinds, rows, dim = text.shape
    halves = kinds // 2
    cores, _, pairs, seg_rows, _ = latents.shape
    slots = seg_rows - GATE_ROWS
    lat = cores * pairs * slots
    lanes = 128
    steps = peers // groups
    fars = pairs // NEAR
    text_spec = pl.BlockSpec((groups, 2, rows, dim), lambda h, i, *s: (i, h, 0, 0))
    sum_spec = pl.BlockSpec(
        (NEAR, fars, slots, 2 * dim), lambda h, i, p, *s: (0, h ^ (p[0] % 2), 0, 0)
    )
    grid_spec = pltpu.PrefetchScalarGridSpec(
        num_scalar_prefetch=3,
        grid=(halves, steps),
        in_specs=[
            pl.BlockSpec(
                (cores, pl.Squeezed(), pairs, seg_rows, 2 * dim),
                lambda h, i, *s: (0, h, 0, 0, 0),
            ),
            pl.BlockSpec(
                (cores * pairs, lanes), lambda h, i, p, *s: (0, p[0] * peers * rows // MB // lanes)
            ),
            text_spec,
        ],
        out_specs=[text_spec, sum_spec, sum_spec],
        scratch_shapes=[
            pltpu.VMEM((lat, dim + lanes), jnp.bfloat16),
            pltpu.VMEM((lat, dim), jnp.bfloat16),
            pltpu.VMEM((dim, lat), jnp.bfloat16),
            pltpu.VMEM((dim, lat), jnp.bfloat16),
            pltpu.VMEM((1, dim), jnp.float32),
            pltpu.VMEM((lat, dim), jnp.float32),
            pltpu.VMEM((lat, dim), jnp.float32),
            pltpu.VMEM((lat, lanes), jnp.float32),
            pltpu.SMEM((cores * pairs + 1,), jnp.int32),
        ],
    )
    sums = (NEAR, halves * fars, slots, 2 * dim)
    return pl.pallas_call(
        heads_kernel,
        grid_spec=grid_spec,
        out_shape=[
            jax.ShapeDtypeStruct(text.shape, jnp.bfloat16),
            jax.ShapeDtypeStruct(sums, jnp.float32),
            jax.ShapeDtypeStruct(sums, jnp.bfloat16),
        ],
        name="attend_heads",
        compiler_params=pltpu.CompilerParams(vmem_limit_bytes=48 << 20),
        cost_estimate=pl.CostEstimate(
            flops=12 * halves * peers * rows * lat * dim,
            bytes_accessed=8 * halves * peers * rows * dim,
            transcendentals=halves * peers * rows * lat,
        ),
    )(place, text_counts, latent_counts, latents, visible_turned, text)


def add_up(keep, send):
    fars = keep.shape[1] // 2
    pairs = lax.axis_size("z_lo")
    other = lax.ppermute(send, "core", [(0, 1), (1, 0)])
    keep = keep + other.astype(jnp.float32)
    send = keep[1:].astype(jnp.bfloat16)
    keep = keep[0]
    arrived = []
    for near in range(1, NEAR):
        steps = [(i, i ^ near) for i in range(pairs)]
        arrived.append(lax.ppermute(send[near - 1], "z_lo", steps))
    for other in arrived:
        keep = keep + other.astype(jnp.float32)
    send = keep[1:].astype(jnp.bfloat16)
    arrived = []
    for far in (2, 1, 3):
        half, block = far // fars, far % fars
        steps = [
            (2 * i + h, 2 * (i ^ (block * NEAR)) + (h ^ half)) for i in range(pairs) for h in range(2)
        ]
        arrived.append(lax.ppermute(send[far - 1], ("z_lo", "z_hi"), steps))
    keep = keep[0]
    for other in arrived:
        keep = keep + other.astype(jnp.float32)
    return keep.astype(jnp.bfloat16)


def shards(
    queries,
    latent_keys,
    latent_values,
    cotangent,
    gate_logits,
    visibility,
    text_counts,
    latent_counts,
):
    halves = lax.axis_size("z_hi")
    peers = lax.axis_size("x") * lax.axis_size("y")
    dim = latent_keys.shape[1]
    place = lax.axis_index(("z_lo", "core", "z_hi")).astype(jnp.int32).reshape(1)
    text, packed = spread(
        gate_logits, queries, cotangent, latent_keys, latent_values, halves, peers
    )
    text = lax.all_to_all(text, ("x", "y"), split_axis=0, concat_axis=0, tiled=True)
    latents = lax.all_gather(packed, ("z_hi", "z_lo"), axis=0, tiled=True)
    latents = lax.all_gather(latents, "core", axis=0, tiled=True)
    latents = latents.reshape(lax.axis_size("core"), halves, lax.axis_size("z_lo"), *packed.shape)
    out, keep, send = attend_heads(
        place, text_counts, latent_counts, latents, visibility.T, text, groups=8
    )
    out = lax.all_to_all(out, ("x", "y"), split_axis=0, concat_axis=0, tiled=True)
    grads = add_up(keep, send)
    mixed_rows, grad_queries = collect(out)
    return (mixed_rows, grad_queries, grads[:, :dim], grads[:, dim:])


def solution(mesh):
    fine = Mesh(mesh.devices.reshape(8, 2, 2, 4, 4), ("z_lo", "core", "z_hi", "x", "y"))
    seg, head = ("z_lo", "core"), ("z_hi", "x", "y")
    in_specs = (
        P(seg + head, None),
        P(seg, head),
        P(seg, head),
        P(seg + head, None),
        P(head),
        P(),
        P(),
        P(),
    )
    out_specs = (P(seg + head, None), P(seg + head, None), P(seg, head), P(seg, head))
    return jax.shard_map(shards, mesh=fine, in_specs=in_specs, out_specs=out_specs, check_vma=False)
```

```python
import math

import jax
import jax.numpy as jnp
from jax import lax
from jax.experimental import pallas as pl
from jax.experimental.pallas import tpu as pltpu
from jax.sharding import Mesh
from jax.sharding import PartitionSpec as P


MB = 128
HIDDEN = -1e30
GATE_ROWS = 8
NEAR = 4
SUBS = 2
SIZES = (256, 384, 416, 448, 480, 512, 768)


def spread_kernel(
    gate_ref, query_ref, grad_ref, latent_key_ref, latent_value_ref, text_ref, packed_ref
):
    peers, kinds, _, width = text_ref.shape
    slots, dim = latent_key_ref.shape
    for half in range(kinds // 2):
        for peer in range(peers):
            columns = pl.ds((half * peers + peer) * width, width)
            text_ref[peer, 2 * half] = query_ref[:, columns]
            text_ref[peer, 2 * half + 1] = grad_ref[:, columns]
    packed_ref[:slots, :dim] = latent_key_ref[...]
    packed_ref[:slots, dim:] = latent_value_ref[...]
    gate = jnp.broadcast_to(gate_ref[...], (GATE_ROWS, 2 * dim))
    first = gate.astype(jnp.bfloat16).astype(jnp.float32)
    second = (gate - first).astype(jnp.bfloat16).astype(jnp.float32)
    third = gate - first - second
    lane = lax.broadcasted_iota(jnp.int32, gate.shape, 1)
    terms = jnp.where(lane == 0, first, jnp.where(lane == 1, second, third))
    packed_ref[slots:, :] = jnp.where(lane < 3, terms, 0.0).astype(jnp.bfloat16)


def spread(gate_logits, queries, cotangent, latent_keys, latent_values, halves, peers):
    rows, columns = queries.shape
    width = columns // (halves * peers)
    slots, dim = latent_keys.shape
    vmem = pl.BlockSpec(memory_space=pltpu.VMEM)
    return pl.pallas_call(
        spread_kernel,
        in_specs=[vmem] * 5,
        out_specs=[vmem, vmem],
        out_shape=[
            jax.ShapeDtypeStruct((peers, 2 * halves, rows, width), queries.dtype),
            jax.ShapeDtypeStruct((slots + GATE_ROWS, 2 * dim), queries.dtype),
        ],
        name="spread",
        cost_estimate=pl.CostEstimate(
            flops=0, bytes_accessed=8 * rows * columns, transcendentals=0
        ),
    )(gate_logits[:, None], queries, cotangent, latent_keys, latent_values)


def collect_kernel(text_ref, mixed_ref, grad_ref):
    peers, kinds, _, width = text_ref.shape
    for half in range(kinds // 2):
        for peer in range(peers):
            columns = pl.ds((half * peers + peer) * width, width)
            mixed_ref[:, columns] = text_ref[peer, 2 * half]
            grad_ref[:, columns] = text_ref[peer, 2 * half + 1]


def collect(text):
    peers, kinds, rows, width = text.shape
    columns = kinds // 2 * peers * width
    whole = jax.ShapeDtypeStruct((rows, columns), text.dtype)
    return pl.pallas_call(
        collect_kernel,
        out_shape=[whole, whole],
        name="collect",
        compiler_params=pltpu.CompilerParams(vmem_limit_bytes=12 << 20),
        cost_estimate=pl.CostEstimate(
            flops=0, bytes_accessed=8 * rows * columns, transcendentals=0
        ),
    )(text)


def heads_kernel(
    place_ref,
    text_counts_ref,
    latent_counts_ref,
    latent_ref,
    visible_ref,
    text_ref,
    out_ref,
    keep_ref,
    send_ref,
    key_ref,
    value_ref,
    key_turned_ref,
    value_turned_ref,
    gate_ref,
    key_sum_ref,
    value_sum_ref,
    hidden_ref,
    starts_ref,
):
    step = pl.program_id(1)
    steps = pl.num_programs(1)
    groups, _, rows, dim = text_ref.shape
    cores, pairs, seg_rows, _ = latent_ref.shape
    segments = cores * pairs
    slots = seg_rows - GATE_ROWS
    lanes = visible_ref.shape[1]
    block_rows = groups * rows
    scaling = 1.0 / math.sqrt(dim)
    to_power = scaling * math.log2(math.e)
    seg_index = place_ref[0] // 2
    half_index = place_ref[0] % 2

    @pl.when(step == 0)
    def _():
        key_sum_ref[...] = jnp.zeros_like(key_sum_ref)
        value_sum_ref[...] = jnp.zeros_like(value_sum_ref)
        hidden_ref[...] = jnp.full(hidden_ref.shape, HIDDEN, jnp.float32)
        start = 0
        for s in range(segments):
            at = pl.ds(start, slots)
            latent = latent_ref.at[s % cores, s // cores]
            count = jnp.where(s <= seg_index, latent_counts_ref[s], 0)
            key_sum_ref[at, :] = latent[:slots, :dim].astype(jnp.float32)
            value_sum_ref[at, :] = latent[:slots, dim:].astype(jnp.float32)
            slot_ok = lax.broadcasted_iota(jnp.int32, (slots, lanes), 0) < count
            seen = jnp.broadcast_to(visible_ref[s : s + 1, :] > 0, (slots, lanes))
            hidden_ref[at, :] = jnp.where(slot_ok & seen, 0.0, HIDDEN)
            starts_ref[s] = jnp.asarray(start, jnp.int32)
            start = start + count
        starts_ref[segments] = start
        key_ref[:, :dim] = key_sum_ref[...].astype(jnp.bfloat16)
        key_ref[:, dim:] = hidden_ref[...].astype(jnp.bfloat16)
        value_ref[...] = value_sum_ref[...].astype(jnp.bfloat16)
        key_turned_ref[...] = key_sum_ref[...].T.astype(jnp.bfloat16)
        value_turned_ref[...] = value_sum_ref[...].T.astype(jnp.bfloat16)
        terms = latent_ref[0, 0, slots:, :dim].astype(jnp.float32)[0:1, :]
        gate_ref[...] = jnp.tanh(jnp.broadcast_to(jnp.sum(terms, axis=1, keepdims=True), (1, dim)))
        key_sum_ref[...] = jnp.zeros_like(key_sum_ref)
        value_sum_ref[...] = jnp.zeros_like(value_sum_ref)

    own_count = text_counts_ref[seg_index] - half_index * (steps * block_rows)
    first_block = (place_ref[0] * (steps * groups)) % lanes
    first_row = step * block_rows
    gate = gate_ref[...]
    turned = (((1,), (1,)), ((), ()))
    sub_groups = groups // SUBS
    sub_rows = sub_groups * rows
    lane_of = lax.broadcasted_iota(jnp.int32, (1, lanes), 1)
    row_of = lax.broadcasted_iota(jnp.int32, (1, sub_rows), 1)

    def score(sub, size):
        query = text_ref[sub * sub_groups : (sub + 1) * sub_groups, 0].reshape(sub_rows, dim)
        own_block = first_block + step * groups + sub * sub_groups
        picks = []
        for g in range(sub_groups):
            pick = jnp.where(lane_of == own_block + g, 1.0, 0.0).astype(jnp.bfloat16)
            picks.append(jnp.broadcast_to(pick, (rows, lanes)))
        asked = jnp.concatenate([query, jnp.concatenate(picks, axis=0)], axis=1)
        return lax.dot_general(key_ref[:size], asked, turned, preferred_element_type=jnp.float32)

    def weigh(scores):
        top = jnp.max(scores, axis=0, keepdims=True)
        powers = jnp.exp2((scores - top) * to_power)
        total = jnp.sum(powers, axis=0, keepdims=True)
        return (powers * (1.0 / total)).astype(jnp.bfloat16)

    def finish(sub, size, weights):
        at = slice(sub * sub_groups, (sub + 1) * sub_groups)
        first = first_row + sub * sub_rows
        query = text_ref[at, 0].reshape(sub_rows, dim)
        grad = text_ref[at, 1].reshape(sub_rows, dim)
        gate_of = jnp.where(row_of + first < own_count, gate[:, 0:1], 0.0)
        grad_out = (grad.T.astype(jnp.float32) * gate_of).astype(jnp.bfloat16)
        attended = jnp.dot(
            value_turned_ref[:, :size], weights, preferred_element_type=jnp.float32
        )
        attended = attended.astype(jnp.bfloat16).astype(jnp.float32)
        mixed = attended * gate_of
        out_ref[at, 0] = mixed.astype(jnp.bfloat16).T.reshape(sub_groups, rows, dim)
        delta = jnp.sum(grad_out.astype(jnp.float32) * attended, axis=0, keepdims=True)
        grad_weights = jnp.dot(value_ref[:size], grad_out, preferred_element_type=jnp.float32)
        grad_scores = weights * (grad_weights - delta).astype(jnp.bfloat16)
        grad_query = (
            jnp.dot(key_turned_ref[:, :size], grad_scores, preferred_element_type=jnp.float32)
            * scaling
        )
        out_ref[at, 1] = grad_query.astype(jnp.bfloat16).T.reshape(sub_groups, rows, dim)
        key_sum_ref[:size] += jnp.dot(grad_scores, query, preferred_element_type=jnp.float32)
        value_sum_ref[:size] += lax.dot_general(
            weights, grad_out, turned, preferred_element_type=jnp.float32
        )

    seen_latents = starts_ref[segments]
    for smaller, size in zip((0,) + SIZES, SIZES):

        @pl.when((seen_latents > smaller) & (seen_latents <= size))
        def _():
            ahead = score(0, size)
            for sub in range(SUBS):
                weights = weigh(ahead)
                if sub + 1 < SUBS:
                    ahead = score(sub + 1, size)
                finish(sub, size, weights)

    @pl.when(step == steps - 1)
    def _():
        core_index = seg_index % cores
        pair_index = seg_index // cores
        slot = lax.broadcasted_iota(jnp.int32, (slots, dim), 0)
        for near in range(NEAR):
            for far in range(pairs // NEAR):
                pair = pair_index ^ (far * NEAR + near)
                for ref, core in ((keep_ref, core_index), (send_ref, 1 - core_index)):
                    segment = pair * cores + core
                    at = pl.ds(starts_ref[segment], slots)
                    own = slot < starts_ref[segment + 1] - starts_ref[segment]
                    key_part = jnp.where(own, key_sum_ref[at, :] * scaling, 0.0)
                    value_part = jnp.where(own, value_sum_ref[at, :], 0.0)
                    ref[near, far, :, :dim] = key_part.astype(ref.dtype)
                    ref[near, far, :, dim:] = value_part.astype(ref.dtype)


def attend_heads(place, text_counts, latent_counts, latents, visible_turned, text, groups):
    peers, kinds, rows, dim = text.shape
    halves = kinds // 2
    cores, _, pairs, seg_rows, _ = latents.shape
    slots = seg_rows - GATE_ROWS
    lat = cores * pairs * slots
    lanes = 128
    steps = peers // groups
    fars = pairs // NEAR
    text_spec = pl.BlockSpec((groups, 2, rows, dim), lambda h, i, *s: (i, h, 0, 0))
    sum_spec = pl.BlockSpec(
        (NEAR, fars, slots, 2 * dim), lambda h, i, p, *s: (0, h ^ (p[0] % 2), 0, 0)
    )
    grid_spec = pltpu.PrefetchScalarGridSpec(
        num_scalar_prefetch=3,
        grid=(halves, steps),
        in_specs=[
            pl.BlockSpec(
                (cores, pl.Squeezed(), pairs, seg_rows, 2 * dim),
                lambda h, i, *s: (0, h, 0, 0, 0),
            ),
            pl.BlockSpec(
                (cores * pairs, lanes), lambda h, i, p, *s: (0, p[0] * peers * rows // MB // lanes)
            ),
            text_spec,
        ],
        out_specs=[text_spec, sum_spec, sum_spec],
        scratch_shapes=[
            pltpu.VMEM((lat, dim + lanes), jnp.bfloat16),
            pltpu.VMEM((lat, dim), jnp.bfloat16),
            pltpu.VMEM((dim, lat), jnp.bfloat16),
            pltpu.VMEM((dim, lat), jnp.bfloat16),
            pltpu.VMEM((1, dim), jnp.float32),
            pltpu.VMEM((lat, dim), jnp.float32),
            pltpu.VMEM((lat, dim), jnp.float32),
            pltpu.VMEM((lat, lanes), jnp.float32),
            pltpu.SMEM((cores * pairs + 1,), jnp.int32),
        ],
    )
    sums = (NEAR, halves * fars, slots, 2 * dim)
    return pl.pallas_call(
        heads_kernel,
        grid_spec=grid_spec,
        out_shape=[
            pltpu.HBM(text.shape, jnp.bfloat16),
            pltpu.HBM(sums, jnp.float32),
            jax.ShapeDtypeStruct(sums, jnp.bfloat16),
        ],
        name="attend_heads",
        compiler_params=pltpu.CompilerParams(vmem_limit_bytes=24 << 20),
        cost_estimate=pl.CostEstimate(
            flops=12 * halves * peers * rows * lat * dim,
            bytes_accessed=8 * halves * peers * rows * dim,
            transcendentals=halves * peers * rows * lat,
        ),
    )(place, text_counts, latent_counts, latents, visible_turned, text)


def add_up(keep, send):
    fars = keep.shape[1] // 2
    pairs = lax.axis_size("z_lo")
    other = lax.ppermute(send, "core", [(0, 1), (1, 0)])
    keep = keep + other.astype(jnp.float32)
    send = keep[1:].astype(jnp.bfloat16)
    keep = keep[0]
    arrived = []
    for near in range(1, NEAR):
        steps = [(i, i ^ near) for i in range(pairs)]
        arrived.append(lax.ppermute(send[near - 1], "z_lo", steps))
    for other in arrived:
        keep = keep + other.astype(jnp.float32)
    send = keep[1:].astype(jnp.bfloat16)
    arrived = []
    for far in (2, 1, 3):
        half, block = far // fars, far % fars
        steps = [
            (2 * i + h, 2 * (i ^ (block * NEAR)) + (h ^ half)) for i in range(pairs) for h in range(2)
        ]
        arrived.append(lax.ppermute(send[far - 1], ("z_lo", "z_hi"), steps))
    keep = keep[0]
    for other in arrived:
        keep = keep + other.astype(jnp.float32)
    return keep.astype(jnp.bfloat16)


def shards(
    queries,
    latent_keys,
    latent_values,
    cotangent,
    gate_logits,
    visibility,
    text_counts,
    latent_counts,
):
    halves = lax.axis_size("z_hi")
    peers = lax.axis_size("x") * lax.axis_size("y")
    dim = latent_keys.shape[1]
    place = lax.axis_index(("z_lo", "core", "z_hi")).astype(jnp.int32).reshape(1)
    text, packed = spread(
        gate_logits, queries, cotangent, latent_keys, latent_values, halves, peers
    )
    text = lax.all_to_all(text, ("x", "y"), split_axis=0, concat_axis=0, tiled=True)
    latents = lax.all_gather(packed, ("z_hi", "z_lo"), axis=0, tiled=True)
    latents = lax.all_gather(latents, "core", axis=0, tiled=True)
    latents = latents.reshape(lax.axis_size("core"), halves, lax.axis_size("z_lo"), *packed.shape)
    out, keep, send = attend_heads(
        place, text_counts, latent_counts, latents, visibility.T, text, groups=8
    )
    out = lax.all_to_all(out, ("x", "y"), split_axis=0, concat_axis=0, tiled=True)
    grads = add_up(keep, send)
    mixed_rows, grad_queries = collect(out)
    return (mixed_rows, grad_queries, grads[:, :dim], grads[:, dim:])


def solution(mesh):
    fine = Mesh(mesh.devices.reshape(8, 2, 2, 4, 4), ("z_lo", "core", "z_hi", "x", "y"))
    seg, head = ("z_lo", "core"), ("z_hi", "x", "y")
    in_specs = (
        P(seg + head, None),
        P(seg, head),
        P(seg, head),
        P(seg + head, None),
        P(head),
        P(),
        P(),
        P(),
    )
    out_specs = (P(seg + head, None), P(seg + head, None), P(seg, head), P(seg, head))
    return jax.shard_map(shards, mesh=fine, in_specs=in_specs, out_specs=out_specs, check_vma=False)
```

```python
import math

import jax
import jax.numpy as jnp
from jax import lax
from jax.experimental import pallas as pl
from jax.experimental.pallas import tpu as pltpu
from jax.sharding import Mesh
from jax.sharding import PartitionSpec as P


MB = 128
HIDDEN = -1e30
GATE_ROWS = 8
NEAR = 4
SUBS = 2
SIZES = (256, 384, 416, 448, 480, 512, 768)


def spread_kernel(
    gate_ref, query_ref, grad_ref, latent_key_ref, latent_value_ref, text_ref, packed_ref
):
    peers, kinds, _, width = text_ref.shape
    slots, dim = latent_key_ref.shape
    for half in range(kinds // 2):
        for peer in range(peers):
            columns = pl.ds((half * peers + peer) * width, width)
            text_ref[peer, 2 * half] = query_ref[:, columns]
            text_ref[peer, 2 * half + 1] = grad_ref[:, columns]
    packed_ref[:slots, :dim] = latent_key_ref[...]
    packed_ref[:slots, dim:] = latent_value_ref[...]
    gate = jnp.broadcast_to(gate_ref[...], (GATE_ROWS, 2 * dim))
    first = gate.astype(jnp.bfloat16).astype(jnp.float32)
    second = (gate - first).astype(jnp.bfloat16).astype(jnp.float32)
    third = gate - first - second
    lane = lax.broadcasted_iota(jnp.int32, gate.shape, 1)
    terms = jnp.where(lane == 0, first, jnp.where(lane == 1, second, third))
    packed_ref[slots:, :] = jnp.where(lane < 3, terms, 0.0).astype(jnp.bfloat16)


def spread(gate_logits, queries, cotangent, latent_keys, latent_values, halves, peers):
    rows, columns = queries.shape
    width = columns // (halves * peers)
    slots, dim = latent_keys.shape
    vmem = pl.BlockSpec(memory_space=pltpu.VMEM)
    return pl.pallas_call(
        spread_kernel,
        in_specs=[vmem] * 5,
        out_specs=[vmem, vmem],
        out_shape=[
            jax.ShapeDtypeStruct((peers, 2 * halves, rows, width), queries.dtype),
            jax.ShapeDtypeStruct((slots + GATE_ROWS, 2 * dim), queries.dtype),
        ],
        name="spread",
        cost_estimate=pl.CostEstimate(
            flops=0, bytes_accessed=8 * rows * columns, transcendentals=0
        ),
    )(gate_logits[:, None], queries, cotangent, latent_keys, latent_values)


def collect_kernel(text_ref, mixed_ref, grad_ref):
    peers, kinds, _, width = text_ref.shape
    for half in range(kinds // 2):
        for peer in range(peers):
            columns = pl.ds((half * peers + peer) * width, width)
            mixed_ref[:, columns] = text_ref[peer, 2 * half]
            grad_ref[:, columns] = text_ref[peer, 2 * half + 1]


def collect(text):
    peers, kinds, rows, width = text.shape
    columns = kinds // 2 * peers * width
    whole = jax.ShapeDtypeStruct((rows, columns), text.dtype)
    return pl.pallas_call(
        collect_kernel,
        out_shape=[whole, whole],
        name="collect",
        compiler_params=pltpu.CompilerParams(vmem_limit_bytes=12 << 20),
        cost_estimate=pl.CostEstimate(
            flops=0, bytes_accessed=8 * rows * columns, transcendentals=0
        ),
    )(text)


def heads_kernel(
    place_ref,
    text_counts_ref,
    latent_counts_ref,
    latent_ref,
    visible_ref,
    text_ref,
    out_ref,
    keep_ref,
    send_ref,
    key_ref,
    value_ref,
    key_turned_ref,
    value_turned_ref,
    gate_ref,
    key_sum_ref,
    value_sum_ref,
    hidden_ref,
    starts_ref,
):
    step = pl.program_id(1)
    steps = pl.num_programs(1)
    groups, _, rows, dim = text_ref.shape
    cores, pairs, seg_rows, _ = latent_ref.shape
    segments = cores * pairs
    slots = seg_rows - GATE_ROWS
    lanes = visible_ref.shape[1]
    block_rows = groups * rows
    scaling = 1.0 / math.sqrt(dim)
    to_power = scaling * math.log2(math.e)
    seg_index = place_ref[0] // 2
    half_index = place_ref[0] % 2

    @pl.when(step == 0)
    def _():
        key_sum_ref[...] = jnp.zeros_like(key_sum_ref)
        value_sum_ref[...] = jnp.zeros_like(value_sum_ref)
        hidden_ref[...] = jnp.full(hidden_ref.shape, HIDDEN, jnp.float32)
        start = 0
        for s in range(segments):
            at = pl.ds(start, slots)
            latent = latent_ref.at[s % cores, s // cores]
            count = jnp.where(s <= seg_index, latent_counts_ref[s], 0)
            key_sum_ref[at, :] = latent[:slots, :dim].astype(jnp.float32)
            value_sum_ref[at, :] = latent[:slots, dim:].astype(jnp.float32)
            slot_ok = lax.broadcasted_iota(jnp.int32, (slots, lanes), 0) < count
            seen = jnp.broadcast_to(visible_ref[s : s + 1, :] > 0, (slots, lanes))
            hidden_ref[at, :] = jnp.where(slot_ok & seen, 0.0, HIDDEN)
            starts_ref[s] = jnp.asarray(start, jnp.int32)
            start = start + count
        starts_ref[segments] = start
        key_ref[:, :dim] = key_sum_ref[...].astype(jnp.bfloat16)
        key_ref[:, dim:] = hidden_ref[...].astype(jnp.bfloat16)
        value_ref[...] = value_sum_ref[...].astype(jnp.bfloat16)
        key_turned_ref[...] = key_sum_ref[...].T.astype(jnp.bfloat16)
        value_turned_ref[...] = value_sum_ref[...].T.astype(jnp.bfloat16)
        terms = latent_ref[0, 0, slots:, :dim].astype(jnp.float32)[0:1, :]
        gate_ref[...] = jnp.tanh(jnp.broadcast_to(jnp.sum(terms, axis=1, keepdims=True), (1, dim)))
        key_sum_ref[...] = jnp.zeros_like(key_sum_ref)
        value_sum_ref[...] = jnp.zeros_like(value_sum_ref)

    own_count = text_counts_ref[seg_index] - half_index * (steps * block_rows)
    first_block = (place_ref[0] * (steps * groups)) % lanes
    first_row = step * block_rows
    gate = gate_ref[...]
    turned = (((1,), (1,)), ((), ()))
    sub_groups = groups // SUBS
    sub_rows = sub_groups * rows
    lane_of = lax.broadcasted_iota(jnp.int32, (1, lanes), 1)
    row_of = lax.broadcasted_iota(jnp.int32, (1, sub_rows), 1)

    def score(sub, size):
        query = text_ref[sub * sub_groups : (sub + 1) * sub_groups, 0].reshape(sub_rows, dim)
        own_block = first_block + step * groups + sub * sub_groups
        picks = []
        for g in range(sub_groups):
            pick = jnp.where(lane_of == own_block + g, 1.0, 0.0).astype(jnp.bfloat16)
            picks.append(jnp.broadcast_to(pick, (rows, lanes)))
        asked = jnp.concatenate([query, jnp.concatenate(picks, axis=0)], axis=1)
        return lax.dot_general(key_ref[:size], asked, turned, preferred_element_type=jnp.float32)

    def weigh(scores):
        top = jnp.max(scores, axis=0, keepdims=True)
        powers = jnp.exp2((scores - top) * to_power)
        total = jnp.sum(powers, axis=0, keepdims=True)
        return (powers * (1.0 / total)).astype(jnp.bfloat16)

    def finish(sub, size, weights):
        at = slice(sub * sub_groups, (sub + 1) * sub_groups)
        first = first_row + sub * sub_rows
        query = text_ref[at, 0].reshape(sub_rows, dim)
        grad = text_ref[at, 1].reshape(sub_rows, dim)
        gate_of = jnp.where(row_of + first < own_count, gate[:, 0:1], 0.0)
        grad_out = (grad.T.astype(jnp.float32) * gate_of).astype(jnp.bfloat16)
        attended = jnp.dot(
            value_turned_ref[:, :size], weights, preferred_element_type=jnp.float32
        )
        attended = attended.astype(jnp.bfloat16).astype(jnp.float32)
        mixed = attended * gate_of
        out_ref[at, 0] = mixed.astype(jnp.bfloat16).T.reshape(sub_groups, rows, dim)
        delta = jnp.sum(grad_out.astype(jnp.float32) * attended, axis=0, keepdims=True)
        grad_weights = jnp.dot(value_ref[:size], grad_out, preferred_element_type=jnp.float32)
        grad_scores = weights * (grad_weights - delta).astype(jnp.bfloat16)
        grad_query = (
            jnp.dot(key_turned_ref[:, :size], grad_scores, preferred_element_type=jnp.float32)
            * scaling
        )
        out_ref[at, 1] = grad_query.astype(jnp.bfloat16).T.reshape(sub_groups, rows, dim)
        key_sum_ref[:size] += jnp.dot(grad_scores, query, preferred_element_type=jnp.float32)
        value_sum_ref[:size] += lax.dot_general(
            weights, grad_out, turned, preferred_element_type=jnp.float32
        )

    seen_latents = starts_ref[segments]
    for smaller, size in zip((0,) + SIZES, SIZES):

        @pl.when((seen_latents > smaller) & (seen_latents <= size))
        def _():
            ahead = score(0, size)
            for sub in range(SUBS):
                weights = weigh(ahead)
                if sub + 1 < SUBS:
                    ahead = score(sub + 1, size)
                finish(sub, size, weights)

    @pl.when(step == steps - 1)
    def _():
        core_index = seg_index % cores
        pair_index = seg_index // cores
        fars = pairs // NEAR
        slot = lax.broadcasted_iota(jnp.int32, (slots, dim), 0)
        for near in range(NEAR):
            for block in range(fars):
                pair = block * NEAR + ((pair_index % NEAR) ^ near)
                shift = (pl.program_id(0) - half_index) * fars + block - pair_index // NEAR
                shift = (shift + keep_ref.shape[1]) % keep_ref.shape[1]
                for ref, core in ((keep_ref, core_index), (send_ref, 1 - core_index)):
                    segment = pair * cores + core
                    at = pl.ds(starts_ref[segment], slots)
                    own = slot < starts_ref[segment + 1] - starts_ref[segment]
                    key_part = jnp.where(own, key_sum_ref[at, :] * scaling, 0.0)
                    value_part = jnp.where(own, value_sum_ref[at, :], 0.0)
                    ref[near, shift, :, :dim] = key_part.astype(ref.dtype)
                    ref[near, shift, :, dim:] = value_part.astype(ref.dtype)


def attend_heads(place, text_counts, latent_counts, latents, visible_turned, text, groups):
    peers, kinds, rows, dim = text.shape
    halves = kinds // 2
    cores, _, pairs, seg_rows, _ = latents.shape
    slots = seg_rows - GATE_ROWS
    lat = cores * pairs * slots
    lanes = 128
    steps = peers // groups
    fars = pairs // NEAR
    text_spec = pl.BlockSpec((groups, 2, rows, dim), lambda h, i, *s: (i, h, 0, 0))
    sum_spec = pl.BlockSpec((NEAR, halves * fars, slots, 2 * dim), lambda h, i, *s: (0, 0, 0, 0))
    grid_spec = pltpu.PrefetchScalarGridSpec(
        num_scalar_prefetch=3,
        grid=(halves, steps),
        in_specs=[
            pl.BlockSpec(
                (cores, pl.Squeezed(), pairs, seg_rows, 2 * dim),
                lambda h, i, *s: (0, h, 0, 0, 0),
            ),
            pl.BlockSpec(
                (cores * pairs, lanes), lambda h, i, p, *s: (0, p[0] * peers * rows // MB // lanes)
            ),
            text_spec,
        ],
        out_specs=[text_spec, sum_spec, sum_spec],
        scratch_shapes=[
            pltpu.VMEM((lat, dim + lanes), jnp.bfloat16),
            pltpu.VMEM((lat, dim), jnp.bfloat16),
            pltpu.VMEM((dim, lat), jnp.bfloat16),
            pltpu.VMEM((dim, lat), jnp.bfloat16),
            pltpu.VMEM((1, dim), jnp.float32),
            pltpu.VMEM((lat, dim), jnp.float32),
            pltpu.VMEM((lat, dim), jnp.float32),
            pltpu.VMEM((lat, lanes), jnp.float32),
            pltpu.SMEM((cores * pairs + 1,), jnp.int32),
        ],
    )
    sums = (NEAR, halves * fars, slots, 2 * dim)
    return pl.pallas_call(
        heads_kernel,
        grid_spec=grid_spec,
        out_shape=[
            pltpu.HBM(text.shape, jnp.bfloat16),
            jax.ShapeDtypeStruct(sums, jnp.bfloat16),
            jax.ShapeDtypeStruct(sums, jnp.bfloat16),
        ],
        name="attend_heads",
        compiler_params=pltpu.CompilerParams(vmem_limit_bytes=24 << 20),
        cost_estimate=pl.CostEstimate(
            flops=12 * halves * peers * rows * lat * dim,
            bytes_accessed=8 * halves * peers * rows * dim,
            transcendentals=halves * peers * rows * lat,
        ),
    )(place, text_counts, latent_counts, latents, visible_turned, text)


def add_up(keep, send):
    pairs = lax.axis_size("z_lo")
    other = lax.ppermute(send, "core", [(0, 1), (1, 0)])
    keep = keep.astype(jnp.float32) + other.astype(jnp.float32)
    send = keep[1:].astype(jnp.bfloat16)
    keep = keep[0]
    arrived = []
    for near in range(1, NEAR):
        steps = [(i, i ^ near) for i in range(pairs)]
        arrived.append(lax.ppermute(send[near - 1], "z_lo", steps))
    for other in arrived:
        keep = keep + other.astype(jnp.float32)
    chips = pairs * lax.axis_size("z_hi")

    def shift(piece, by):
        flat = lambda z: z % pairs * 2 + z // pairs
        steps = [(flat(z), flat((z + by) % chips)) for z in range(chips)]
        return lax.ppermute(piece.astype(jnp.bfloat16), ("z_lo", "z_hi"), steps)

    passing = shift(keep[2], NEAR)
    left = shift(keep[3], -NEAR)
    right = shift(keep[1] + passing.astype(jnp.float32), NEAR)
    return (keep[0] + left.astype(jnp.float32) + right.astype(jnp.float32)).astype(jnp.bfloat16)


def shards(
    queries,
    latent_keys,
    latent_values,
    cotangent,
    gate_logits,
    visibility,
    text_counts,
    latent_counts,
):
    halves = lax.axis_size("z_hi")
    peers = lax.axis_size("x") * lax.axis_size("y")
    dim = latent_keys.shape[1]
    place = lax.axis_index(("z_lo", "core", "z_hi")).astype(jnp.int32).reshape(1)
    text, packed = spread(
        gate_logits, queries, cotangent, latent_keys, latent_values, halves, peers
    )
    text = lax.all_to_all(text, ("x", "y"), split_axis=0, concat_axis=0, tiled=True)
    latents = lax.all_gather(packed, ("z_hi", "z_lo"), axis=0, tiled=True)
    latents = lax.all_gather(latents, "core", axis=0, tiled=True)
    latents = latents.reshape(lax.axis_size("core"), halves, lax.axis_size("z_lo"), *packed.shape)
    out, keep, send = attend_heads(
        place, text_counts, latent_counts, latents, visibility.T, text, groups=8
    )
    out = lax.all_to_all(out, ("x", "y"), split_axis=0, concat_axis=0, tiled=True)
    grads = add_up(keep, send)
    mixed_rows, grad_queries = collect(out)
    return (mixed_rows, grad_queries, grads[:, :dim], grads[:, dim:])


def solution(mesh):
    fine = Mesh(mesh.devices.reshape(8, 2, 2, 4, 4), ("z_lo", "core", "z_hi", "x", "y"))
    seg, head = ("z_lo", "core"), ("z_hi", "x", "y")
    in_specs = (
        P(seg + head, None),
        P(seg, head),
        P(seg, head),
        P(seg + head, None),
        P(head),
        P(),
        P(),
        P(),
    )
    out_specs = (P(seg + head, None), P(seg + head, None), P(seg, head), P(seg, head))
    return jax.shard_map(shards, mesh=fine, in_specs=in_specs, out_specs=out_specs, check_vma=False)
```

```python
import math

import jax
import jax.numpy as jnp
from jax import lax
from jax.experimental import pallas as pl
from jax.experimental.pallas import tpu as pltpu
from jax.sharding import Mesh
from jax.sharding import PartitionSpec as P


MB = 128
HIDDEN = -1e30
GATE_ROWS = 8
NEAR = 4
SUBS = 2
SIZES = (256, 384, 416, 448, 480, 512, 768)


def spread_kernel(
    gate_ref, query_ref, grad_ref, latent_key_ref, latent_value_ref, text_ref, packed_ref
):
    peers, kinds, _, width = text_ref.shape
    slots, dim = latent_key_ref.shape
    for half in range(kinds // 2):
        for peer in range(peers):
            columns = pl.ds((half * peers + peer) * width, width)
            text_ref[peer, 2 * half] = query_ref[:, columns]
            text_ref[peer, 2 * half + 1] = grad_ref[:, columns]
    packed_ref[:slots, :dim] = latent_key_ref[...]
    packed_ref[:slots, dim:] = latent_value_ref[...]
    gate = jnp.broadcast_to(gate_ref[...], (GATE_ROWS, 2 * dim))
    first = gate.astype(jnp.bfloat16).astype(jnp.float32)
    second = (gate - first).astype(jnp.bfloat16).astype(jnp.float32)
    third = gate - first - second
    lane = lax.broadcasted_iota(jnp.int32, gate.shape, 1)
    terms = jnp.where(lane == 0, first, jnp.where(lane == 1, second, third))
    packed_ref[slots:, :] = jnp.where(lane < 3, terms, 0.0).astype(jnp.bfloat16)


def spread(gate_logits, queries, cotangent, latent_keys, latent_values, halves, peers):
    rows, columns = queries.shape
    width = columns // (halves * peers)
    slots, dim = latent_keys.shape
    vmem = pl.BlockSpec(memory_space=pltpu.VMEM)
    return pl.pallas_call(
        spread_kernel,
        in_specs=[vmem] * 5,
        out_specs=[vmem, vmem],
        out_shape=[
            jax.ShapeDtypeStruct((peers, 2 * halves, rows, width), queries.dtype),
            jax.ShapeDtypeStruct((slots + GATE_ROWS, 2 * dim), queries.dtype),
        ],
        name="spread",
        cost_estimate=pl.CostEstimate(
            flops=0, bytes_accessed=8 * rows * columns, transcendentals=0
        ),
    )(gate_logits[:, None], queries, cotangent, latent_keys, latent_values)


def collect_kernel(text_ref, mixed_ref, grad_ref):
    peers, kinds, _, width = text_ref.shape
    for half in range(kinds // 2):
        for peer in range(peers):
            columns = pl.ds((half * peers + peer) * width, width)
            mixed_ref[:, columns] = text_ref[peer, 2 * half]
            grad_ref[:, columns] = text_ref[peer, 2 * half + 1]


def collect(text):
    peers, kinds, rows, width = text.shape
    columns = kinds // 2 * peers * width
    whole = jax.ShapeDtypeStruct((rows, columns), text.dtype)
    return pl.pallas_call(
        collect_kernel,
        out_shape=[whole, whole],
        name="collect",
        compiler_params=pltpu.CompilerParams(vmem_limit_bytes=12 << 20),
        cost_estimate=pl.CostEstimate(
            flops=0, bytes_accessed=8 * rows * columns, transcendentals=0
        ),
    )(text)


def heads_kernel(
    place_ref,
    text_counts_ref,
    latent_counts_ref,
    latent_ref,
    visible_ref,
    text_ref,
    out_ref,
    keep_ref,
    send_ref,
    key_ref,
    value_ref,
    key_turned_ref,
    value_turned_ref,
    gate_ref,
    key_sum_ref,
    value_sum_ref,
    hidden_ref,
    starts_ref,
):
    step = pl.program_id(1)
    steps = pl.num_programs(1)
    groups, _, rows, dim = text_ref.shape
    cores, pairs, seg_rows, _ = latent_ref.shape
    segments = cores * pairs
    slots = seg_rows - GATE_ROWS
    lanes = visible_ref.shape[1]
    block_rows = groups * rows
    scaling = 1.0 / math.sqrt(dim)
    to_power = scaling * math.log2(math.e)
    seg_index = place_ref[0] // 2
    half_index = place_ref[0] % 2

    @pl.when(step == 0)
    def _():
        key_sum_ref[...] = jnp.zeros_like(key_sum_ref)
        value_sum_ref[...] = jnp.zeros_like(value_sum_ref)
        hidden_ref[...] = jnp.full(hidden_ref.shape, HIDDEN, jnp.float32)
        start = 0
        for s in range(segments):
            at = pl.ds(start, slots)
            latent = latent_ref.at[s % cores, s // cores]
            count = jnp.where(s <= seg_index, latent_counts_ref[s], 0)
            key_sum_ref[at, :] = latent[:slots, :dim].astype(jnp.float32)
            value_sum_ref[at, :] = latent[:slots, dim:].astype(jnp.float32)
            slot_ok = lax.broadcasted_iota(jnp.int32, (slots, lanes), 0) < count
            seen = jnp.broadcast_to(visible_ref[s : s + 1, :] > 0, (slots, lanes))
            hidden_ref[at, :] = jnp.where(slot_ok & seen, 0.0, HIDDEN)
            starts_ref[s] = jnp.asarray(start, jnp.int32)
            start = start + count
        starts_ref[segments] = start
        key_ref[:, :dim] = key_sum_ref[...].astype(jnp.bfloat16)
        key_ref[:, dim:] = hidden_ref[...].astype(jnp.bfloat16)
        value_ref[...] = value_sum_ref[...].astype(jnp.bfloat16)
        key_turned_ref[...] = key_sum_ref[...].T.astype(jnp.bfloat16)
        value_turned_ref[...] = value_sum_ref[...].T.astype(jnp.bfloat16)
        terms = latent_ref[0, 0, slots:, :dim].astype(jnp.float32)[0:1, :]
        gate_ref[...] = jnp.tanh(jnp.broadcast_to(jnp.sum(terms, axis=1, keepdims=True), (1, dim)))
        key_sum_ref[...] = jnp.zeros_like(key_sum_ref)
        value_sum_ref[...] = jnp.zeros_like(value_sum_ref)

    own_count = text_counts_ref[seg_index] - half_index * (steps * block_rows)
    first_block = (place_ref[0] * (steps * groups)) % lanes
    first_row = step * block_rows
    gate = gate_ref[...]
    turned = (((1,), (1,)), ((), ()))
    sub_groups = groups // SUBS
    sub_rows = sub_groups * rows
    lane_of = lax.broadcasted_iota(jnp.int32, (1, lanes), 1)
    row_of = lax.broadcasted_iota(jnp.int32, (1, sub_rows), 1)

    def score(sub, size):
        query = text_ref[sub * sub_groups : (sub + 1) * sub_groups, 0].reshape(sub_rows, dim)
        own_block = first_block + step * groups + sub * sub_groups
        picks = []
        for g in range(sub_groups):
            pick = jnp.where(lane_of == own_block + g, 1.0, 0.0).astype(jnp.bfloat16)
            picks.append(jnp.broadcast_to(pick, (rows, lanes)))
        asked = jnp.concatenate([query, jnp.concatenate(picks, axis=0)], axis=1)
        return lax.dot_general(key_ref[:size], asked, turned, preferred_element_type=jnp.float32)

    def weigh(scores):
        top = jnp.max(scores, axis=0, keepdims=True)
        powers = jnp.exp2((scores - top) * to_power)
        total = jnp.sum(powers, axis=0, keepdims=True)
        return (powers * (1.0 / total)).astype(jnp.bfloat16)

    def finish(sub, size, weights):
        at = slice(sub * sub_groups, (sub + 1) * sub_groups)
        first = first_row + sub * sub_rows
        query = text_ref[at, 0].reshape(sub_rows, dim)
        grad = text_ref[at, 1].reshape(sub_rows, dim)
        gate_of = jnp.where(row_of + first < own_count, gate[:, 0:1], 0.0)
        grad_out = (grad.T.astype(jnp.float32) * gate_of).astype(jnp.bfloat16)
        attended = jnp.dot(
            value_turned_ref[:, :size], weights, preferred_element_type=jnp.float32
        )
        attended = attended.astype(jnp.bfloat16).astype(jnp.float32)
        mixed = attended * gate_of
        out_ref[at, 0] = mixed.astype(jnp.bfloat16).T.reshape(sub_groups, rows, dim)
        delta = jnp.sum(grad_out.astype(jnp.float32) * attended, axis=0, keepdims=True)
        grad_weights = jnp.dot(value_ref[:size], grad_out, preferred_element_type=jnp.float32)
        grad_scores = weights * (grad_weights - delta).astype(jnp.bfloat16)
        grad_query = (
            jnp.dot(key_turned_ref[:, :size], grad_scores, preferred_element_type=jnp.float32)
            * scaling
        )
        out_ref[at, 1] = grad_query.astype(jnp.bfloat16).T.reshape(sub_groups, rows, dim)
        key_sum_ref[:size] += jnp.dot(grad_scores, query, preferred_element_type=jnp.float32)
        value_sum_ref[:size] += lax.dot_general(
            weights, grad_out, turned, preferred_element_type=jnp.float32
        )

    seen_latents = starts_ref[segments]
    for smaller, size in zip((0,) + SIZES, SIZES):

        @pl.when((seen_latents > smaller) & (seen_latents <= size))
        def _():
            ahead = score(0, size)
            for sub in range(SUBS):
                weights = weigh(ahead)
                if sub + 1 < SUBS:
                    ahead = score(sub + 1, size)
                finish(sub, size, weights)

    @pl.when(step == steps - 1)
    def _():
        core_index = seg_index % cores
        pair_index = seg_index // cores
        chips = keep_ref.shape[0] * keep_ref.shape[1]
        slot = lax.broadcasted_iota(jnp.int32, (slots, dim), 0)
        for pair in range(pairs):
            distance = (pl.program_id(0) - half_index) * pairs + pair - pair_index
            distance = (distance + chips) % chips
            near = distance % NEAR
            far = (distance + 1) // NEAR % keep_ref.shape[1]
            for ref, core in ((keep_ref, core_index), (send_ref, 1 - core_index)):
                segment = pair * cores + core
                at = pl.ds(starts_ref[segment], slots)
                own = slot < starts_ref[segment + 1] - starts_ref[segment]
                key_part = jnp.where(own, key_sum_ref[at, :] * scaling, 0.0)
                value_part = jnp.where(own, value_sum_ref[at, :], 0.0)
                ref[near, far, :, :dim] = key_part.astype(ref.dtype)
                ref[near, far, :, dim:] = value_part.astype(ref.dtype)


def attend_heads(place, text_counts, latent_counts, latents, visible_turned, text, groups):
    peers, kinds, rows, dim = text.shape
    halves = kinds // 2
    cores, _, pairs, seg_rows, _ = latents.shape
    slots = seg_rows - GATE_ROWS
    lat = cores * pairs * slots
    lanes = 128
    steps = peers // groups
    fars = pairs // NEAR
    text_spec = pl.BlockSpec((groups, 2, rows, dim), lambda h, i, *s: (i, h, 0, 0))
    sum_spec = pl.BlockSpec((NEAR, halves * fars, slots, 2 * dim), lambda h, i, *s: (0, 0, 0, 0))
    grid_spec = pltpu.PrefetchScalarGridSpec(
        num_scalar_prefetch=3,
        grid=(halves, steps),
        in_specs=[
            pl.BlockSpec(
                (cores, pl.Squeezed(), pairs, seg_rows, 2 * dim),
                lambda h, i, *s: (0, h, 0, 0, 0),
            ),
            pl.BlockSpec(
                (cores * pairs, lanes), lambda h, i, p, *s: (0, p[0] * peers * rows // MB // lanes)
            ),
            text_spec,
        ],
        out_specs=[text_spec, sum_spec, sum_spec],
        scratch_shapes=[
            pltpu.VMEM((lat, dim + lanes), jnp.bfloat16),
            pltpu.VMEM((lat, dim), jnp.bfloat16),
            pltpu.VMEM((dim, lat), jnp.bfloat16),
            pltpu.VMEM((dim, lat), jnp.bfloat16),
            pltpu.VMEM((1, dim), jnp.float32),
            pltpu.VMEM((lat, dim), jnp.float32),
            pltpu.VMEM((lat, dim), jnp.float32),
            pltpu.VMEM((lat, lanes), jnp.float32),
            pltpu.SMEM((cores * pairs + 1,), jnp.int32),
        ],
    )
    sums = (NEAR, halves * fars, slots, 2 * dim)
    return pl.pallas_call(
        heads_kernel,
        grid_spec=grid_spec,
        out_shape=[
            pltpu.HBM(text.shape, jnp.bfloat16),
            jax.ShapeDtypeStruct(sums, jnp.bfloat16),
            jax.ShapeDtypeStruct(sums, jnp.bfloat16),
        ],
        name="attend_heads",
        compiler_params=pltpu.CompilerParams(vmem_limit_bytes=24 << 20),
        cost_estimate=pl.CostEstimate(
            flops=12 * halves * peers * rows * lat * dim,
            bytes_accessed=8 * halves * peers * rows * dim,
            transcendentals=halves * peers * rows * lat,
        ),
    )(place, text_counts, latent_counts, latents, visible_turned, text)


def shift(piece, by):
    pairs = lax.axis_size("z_lo")
    chips = pairs * lax.axis_size("z_hi")
    place = [z % pairs * 2 + z // pairs for z in range(chips)]
    steps = [(place[z], place[(z + by) % chips]) for z in range(chips)]
    return lax.ppermute(piece.astype(jnp.bfloat16), ("z_lo", "z_hi"), steps)


def stage(pieces, by):
    passing = shift(pieces[2], by)
    left = shift(pieces[3], -by)
    right = shift(pieces[1] + passing.astype(jnp.float32), by)
    return pieces[0], left.astype(jnp.float32), right.astype(jnp.float32)


def add_up(keep, send):
    other = lax.ppermute(send, "core", [(0, 1), (1, 0)])
    own, left, right = stage(keep.astype(jnp.float32) + other.astype(jnp.float32), 1)
    own, left, right = stage(own + left + right, NEAR)
    dim = own.shape[1] // 2
    return tuple(
        (own[:, at] + left[:, at] + right[:, at]).astype(jnp.bfloat16)
        for at in (slice(0, dim), slice(dim, None))
    )


def shards(
    queries,
    latent_keys,
    latent_values,
    cotangent,
    gate_logits,
    visibility,
    text_counts,
    latent_counts,
):
    halves = lax.axis_size("z_hi")
    peers = lax.axis_size("x") * lax.axis_size("y")
    place = lax.axis_index(("z_lo", "core", "z_hi")).astype(jnp.int32).reshape(1)
    text, packed = spread(
        gate_logits, queries, cotangent, latent_keys, latent_values, halves, peers
    )
    text = lax.all_to_all(text, ("x", "y"), split_axis=0, concat_axis=0, tiled=True)
    latents = lax.all_gather(packed, ("z_hi", "z_lo"), axis=0, tiled=True)
    latents = lax.all_gather(latents, "core", axis=0, tiled=True)
    latents = latents.reshape(lax.axis_size("core"), halves, lax.axis_size("z_lo"), *packed.shape)
    out, keep, send = attend_heads(
        place, text_counts, latent_counts, latents, visibility.T, text, groups=8
    )
    out = lax.all_to_all(out, ("x", "y"), split_axis=0, concat_axis=0, tiled=True)
    grad_keys, grad_values = add_up(keep, send)
    mixed_rows, grad_queries = collect(out)
    return (mixed_rows, grad_queries, grad_keys, grad_values)


def solution(mesh):
    fine = Mesh(mesh.devices.reshape(8, 2, 2, 4, 4), ("z_lo", "core", "z_hi", "x", "y"))
    seg, head = ("z_lo", "core"), ("z_hi", "x", "y")
    in_specs = (
        P(seg + head, None),
        P(seg, head),
        P(seg, head),
        P(seg + head, None),
        P(head),
        P(),
        P(),
        P(),
    )
    out_specs = (P(seg + head, None), P(seg + head, None), P(seg, head), P(seg, head))
    return jax.shard_map(shards, mesh=fine, in_specs=in_specs, out_specs=out_specs, check_vma=False)
```
